512 devices in a mesh: ctx: 64 (over x, y, core), head: 8 (over z).
Axes of the slice: x: 4, y: 8, z: 8, core: 2. Of those that a mesh axis runs over, the one named last changes fastest.
Arguments:
- queries: bfloat16 [98304, 4096], P(('ctx', 'head')), may hold values from -8 to 8
- keys: bfloat16 [98304, 1024], P(('ctx', 'head')), may hold values from -4 to 4
- values: bfloat16 [98304, 1024], P(('ctx', 'head')), may hold values from -6 to 6
- doc_start: int32 [256], replicated, may hold values from 0 to 768, as said below
- doc_blocks: int32 [256], replicated, may hold values from 0 to 12, as said below
- doc_rank: int32 [256], replicated, may hold values from 0 to 63, as said below
- doc_slot: int32 [256], replicated, may hold values from 0 to 12, as said below
Outputs:
- attended: bfloat16 [98304, 4096], P(('ctx', 'head'))
The draws below stay inside these ranges and needn't reach their ends.
Inputs may be any that keep to these rules, and one draw needn't show every extreme that they name: Entries are listed in packing order: doc_start is the sum of doc_blocks over the earlier entries, so the entries cover the 98304 tokens block by block. `doc_blocks`: an entry may hold 0 blocks. `doc_rank`: each ctx rank is named by exactly 4 entries. The entries that name one rank cover its 12 blocks without gaps or repeats; doc_slot is the first block of each.
All inputs are finite; a program needn't handle non-finite values.
Results may differ from the reference program's by a relative error of at most 0.0036.
Values may be sent and summed in bfloat16 or wider, within the bound.
No kernel may reach another device: no remote copies, remote signals or barrier semaphores. Data moves between devices by JAX's collectives and lax.ppermute only.
A program may use at most 64 MiB of HBM per device.

```python
import math
import jax
import jax.numpy as jnp
from jax import lax

QUERY_HEAD_COUNT = 32
KEY_VALUE_HEADS = 8
HEAD_WIDTH = 128
BLOCK = 128
DOCS_RANK = 4
TOK_DEV = 192
BPR = 12
PACKED_TOKENS = 98304
NDOC = 256
N_CTX = 64
N_HEAD = 8


def doc_lists(key):
    folded = jax.random.fold_in(key, 41)
    document_flows = jax.random.split(folded, 4)
    cut_points = jnp.sort(jax.random.randint(document_flows[0], (N_CTX, DOCS_RANK - 1), 0, BPR + 1), axis=1).astype(jnp.int32)
    boundary = jnp.concatenate([jnp.zeros((N_CTX, 1), jnp.int32), cut_points, jnp.full((N_CTX, 1), BPR, jnp.int32)], axis=1)
    lengths = boundary[:, 1:] - boundary[:, :-1]
    chosen_rank = jax.random.randint(document_flows[1], (), 0, N_CTX)
    chosen_place = jax.random.randint(document_flows[2], (), 0, DOCS_RANK)
    single = jnp.where(jnp.arange(DOCS_RANK, dtype=jnp.int32) == chosen_place, BPR, 0).astype(jnp.int32)
    lengths = jnp.where((jnp.arange(N_CTX, dtype=jnp.int32) == chosen_rank)[:, None], single[None, :], lengths)
    offsets = jnp.cumsum(lengths, axis=1) - lengths
    owners = jnp.broadcast_to(jnp.arange(N_CTX, dtype=jnp.int32)[:, None], (N_CTX, DOCS_RANK))
    packing = jax.random.permutation(document_flows[3], NDOC)
    blocks = lengths.reshape(-1)[packing].astype(jnp.int32)
    slots = offsets.reshape(-1)[packing].astype(jnp.int32)
    ranks = owners.reshape(-1)[packing].astype(jnp.int32)
    starts = (jnp.cumsum(blocks) - blocks).astype(jnp.int32)
    return (starts, blocks, ranks, slots)


def query_key(key):
    folded = jax.random.fold_in(key, 97)
    document_flows = jax.random.split(folded, 2)
    query_draw = jnp.clip(jax.random.normal(document_flows[0], (PACKED_TOKENS, QUERY_HEAD_COUNT * HEAD_WIDTH), jnp.float32), -4.0, 4.0)
    key_sample = jnp.clip(jax.random.normal(document_flows[1], (PACKED_TOKENS, KEY_VALUE_HEADS * HEAD_WIDTH), jnp.float32), -4.0, 4.0)
    return (query_draw, key_sample)


def draw_queries(key, part):
    return query_key(key)[0].astype(jnp.bfloat16)


def draw_keys(key, part):
    return query_key(key)[1].astype(jnp.bfloat16)


def draw_doc_start(key, part):
    return doc_lists(key)[0]


def draw_doc_blocks(key, part):
    return doc_lists(key)[1]


def draw_doc_rank(key, part):
    return doc_lists(key)[2]


def draw_doc_slot(key, part):
    return doc_lists(key)[3]


def shard_levels(rng, dims, cuts, least, top_value):
    level, own = 1.0, jax.random.fold_in(rng, 6)
    for axis_at, parts in cuts:
        heights = jnp.exp(jax.random.uniform(jax.random.fold_in(own, axis_at), (parts,), jnp.float32, least / len(cuts), top_value / len(cuts)))
        level = level * jnp.repeat(heights, dims[axis_at] // parts).reshape([-1 if axis == axis_at else 1 for axis in range(len(dims))])
    return level


def gaussian(key, dims, deviation, limit, shards=(), kind=jnp.bfloat16):
    gain = shard_levels(key, dims, shards, -0.22, 0.18) if shards else 1.0
    array = jax.random.normal(key, dims, jnp.float32) * deviation * gain
    return jnp.minimum(jnp.maximum(array, -limit), limit).astype(kind)


def setup_inputs(seed: int = 0) -> dict:
    splits = jax.random.split(jax.random.key(seed), 8)
    return {
        "queries": draw_queries(jax.random.fold_in(splits[7], 71), 0),
        "keys": draw_keys(jax.random.fold_in(splits[7], 71), 0),
        "values": gaussian(splits[2], (PACKED_TOKENS, KEY_VALUE_HEADS * HEAD_WIDTH), 1.0, 6.0, ((0, 512),)),
        "doc_start": draw_doc_start(jax.random.fold_in(splits[7], 71), 0),
        "doc_blocks": draw_doc_blocks(jax.random.fold_in(splits[7], 71), 0),
        "doc_rank": draw_doc_rank(jax.random.fold_in(splits[7], 71), 0),
        "doc_slot": draw_doc_slot(jax.random.fold_in(splits[7], 71), 0),
    }


def reference(queries, keys, values, doc_start, doc_blocks, doc_rank, doc_slot):
    rows_per_rank = TOK_DEV * N_HEAD
    repeat_factor = QUERY_HEAD_COUNT // KEY_VALUE_HEADS
    local_rows = jnp.arange(rows_per_rank, dtype=jnp.int32)
    entry_list = jnp.arange(doc_start.shape[0], dtype=jnp.int32)
    causal = local_rows[None, :] <= local_rows[:, None]
    scaling = 1.0 / math.sqrt(HEAD_WIDTH)

    def one_rank(rank_id):
        block_ids = local_rows // BLOCK
        matches = ((doc_rank[None, :] == rank_id) & (doc_slot[None, :] <= block_ids[:, None]) & (block_ids[:, None] < (doc_slot + doc_blocks)[None, :])).astype(jnp.int32)
        entry_ids = lax.optimization_barrier(jnp.sum(matches * entry_list[None, :], axis=1))
        offset_rows = lax.optimization_barrier(jnp.sum(matches * (doc_start - doc_slot)[None, :], axis=1)) * BLOCK
        anchor_point = (local_rows + offset_rows).astype(jnp.int32)
        query_matrix = jnp.take(queries, anchor_point, axis=0).astype(jnp.float32)
        query_matrix = query_matrix.reshape(rows_per_rank, KEY_VALUE_HEADS, repeat_factor, HEAD_WIDTH).transpose(1, 2, 0, 3)
        key_matrix = jnp.take(keys, anchor_point, axis=0).astype(jnp.float32).reshape(rows_per_rank, KEY_VALUE_HEADS, HEAD_WIDTH).transpose(1, 0, 2)
        value_matrix = jnp.take(values, anchor_point, axis=0).astype(jnp.float32).reshape(rows_per_rank, KEY_VALUE_HEADS, HEAD_WIDTH).transpose(1, 0, 2)
        allowed = (entry_ids[:, None] == entry_ids[None, :]) & causal

        def one_group(group):
            query_group, key_group, value_group = group
            scores = jnp.einsum('rpd,qd->rpq', query_group, key_group) * scaling
            row_top = lax.optimization_barrier(jnp.max(jnp.where(allowed, scores, -jnp.inf), axis=-1, keepdims=True))
            weights = jnp.where(allowed, jnp.exp(scores - row_top), 0.0)
            totals = lax.optimization_barrier(jnp.sum(weights, axis=-1))
            rounded = lax.optimization_barrier(weights.astype(jnp.bfloat16)).astype(jnp.float32)
            weighted = jnp.einsum('rpq,qd->rpd', rounded, value_group)
            return (weighted / totals[..., None]).astype(jnp.bfloat16)
        outputs = lax.map(one_group, (query_matrix, key_matrix, value_matrix))
        return outputs.transpose(2, 0, 1, 3).reshape(rows_per_rank, QUERY_HEAD_COUNT * HEAD_WIDTH)
    ranked = lax.map(one_rank, jnp.arange(N_CTX, dtype=jnp.int32))
    return ranked.reshape(PACKED_TOKENS, QUERY_HEAD_COUNT * HEAD_WIDTH)
```

```python
import math

import jax
import jax.numpy as jnp
from jax import lax
from jax.experimental import pallas as pl
from jax.experimental.pallas import tpu as pltpu
from jax.sharding import PartitionSpec as P

HEAD_WIDTH = 128
BLOCK = 128
HALF = 64
QUAD = 4
MASKED = -1e30
EXP2_SCALE = math.log2(math.e) / math.sqrt(HEAD_WIDTH)


def attend_kernel(
    lengths, q_ref, kv_hbm, halo_hbm, out_ref, kv_ref, score_ref, top_ref, sum_ref, acc_ref, sems
):
    block = pl.program_id(0)
    heads = q_ref.shape[1] // HEAD_WIDTH
    halo_rows = halo_hbm.shape[0]
    rows = heads * BLOCK

    @pl.when(block == 0)
    def _():
        own = pltpu.make_async_copy(
            kv_hbm, kv_ref.at[pl.ds(halo_rows, kv_hbm.shape[0])], sems.at[0]
        )
        before = pltpu.make_async_copy(halo_hbm, kv_ref.at[pl.ds(0, halo_rows)], sems.at[1])
        own.start()
        before.start()
        own.wait()
        before.wait()

    length = lengths[block]
    chunks = (length + 1) // 2
    last_row = halo_rows + block * BLOCK
    q = jnp.concatenate(
        [q_ref[:, h * HEAD_WIDTH : (h + 1) * HEAD_WIDTH] for h in range(heads)], axis=0
    )

    def scores_of(chunk):
        first = pl.multiple_of(last_row - BLOCK - chunk * 2 * BLOCK, BLOCK)
        keys = kv_ref[pl.ds(first, 2 * BLOCK), :HEAD_WIDTH]
        s = lax.dot_general(q, keys, (((1,), (1,)), ((), ())), preferred_element_type=jnp.float32)
        older = jnp.where(2 * chunk + 2 <= length, s[:, :BLOCK], MASKED)
        return older, s[:, BLOCK:]

    older, newer = scores_of(0)
    row_ids = lax.broadcasted_iota(jnp.int32, (rows, BLOCK), 0) % BLOCK
    col_ids = lax.broadcasted_iota(jnp.int32, (rows, BLOCK), 1)
    newer = jnp.where(col_ids <= row_ids, newer, MASKED)
    score_ref[0, :, :BLOCK] = older
    score_ref[0, :, BLOCK:] = newer
    top_ref[...] = jnp.maximum(older, newer)

    def first_pass(chunk, carry):
        older, newer = scores_of(chunk)
        score_ref[chunk, :, :BLOCK] = older
        score_ref[chunk, :, BLOCK:] = newer
        top_ref[...] = jnp.maximum(top_ref[...], jnp.maximum(older, newer))
        return carry

    lax.fori_loop(1, chunks, first_pass, 0)
    top = jnp.max(top_ref[...], axis=1, keepdims=True) * EXP2_SCALE
    top_ref[...] = jnp.broadcast_to(top, (rows, BLOCK))
    sum_ref[...] = jnp.zeros_like(sum_ref)
    acc_ref[...] = jnp.zeros_like(acc_ref)

    def second_pass(chunk, carry):
        first = pl.multiple_of(last_row - BLOCK - chunk * 2 * BLOCK, BLOCK)
        vals = kv_ref[pl.ds(first, 2 * BLOCK), HEAD_WIDTH:]
        shift = top_ref[...]
        older = jnp.exp2(score_ref[chunk, :, :BLOCK] * EXP2_SCALE - shift)
        newer = jnp.exp2(score_ref[chunk, :, BLOCK:] * EXP2_SCALE - shift)
        sum_ref[...] += older + newer
        weights = jnp.concatenate(
            [older.astype(jnp.bfloat16), newer.astype(jnp.bfloat16)], axis=1
        )
        acc_ref[...] += jnp.dot(weights, vals, preferred_element_type=jnp.float32)
        return carry

    lax.fori_loop(0, chunks, second_pass, 0)
    totals = jnp.sum(sum_ref[...], axis=1, keepdims=True)
    out = acc_ref[...] / totals
    low = lax.broadcasted_iota(jnp.int32, (HALF, HEAD_WIDTH), 0) % (2 * QUAD) < QUAD
    for h in range(heads):
        upper = out[h * BLOCK : h * BLOCK + HALF]
        lower = out[h * BLOCK + HALF : (h + 1) * BLOCK]
        even = jnp.where(low, upper, pltpu.roll(lower, QUAD, 0))
        odd = jnp.where(low, pltpu.roll(upper, HALF - QUAD, 0), lower)
        for k in range(HALF // (2 * QUAD)):
            tile = slice(2 * QUAD * k, 2 * QUAD * (k + 1))
            out_ref[2 * k * heads + h, 0] = even[tile].astype(jnp.bfloat16)
            out_ref[(2 * k + 1) * heads + h, 0] = odd[tile].astype(jnp.bfloat16)


def attend(lengths, q, kv, halo):
    blocks = q.shape[0] // BLOCK
    heads = q.shape[1] // HEAD_WIDTH
    units = HALF // QUAD * heads
    chunks = (blocks + 1) // 2
    rows = heads * BLOCK
    return pl.pallas_call(
        attend_kernel,
        out_shape=jax.ShapeDtypeStruct((units, blocks, 2 * QUAD, HEAD_WIDTH), jnp.bfloat16),
        grid_spec=pltpu.PrefetchScalarGridSpec(
            num_scalar_prefetch=1,
            grid=(blocks,),
            in_specs=[
                pl.BlockSpec((BLOCK, q.shape[1]), lambda b, lengths: (b, 0)),
                pl.BlockSpec(memory_space=pl.ANY),
                pl.BlockSpec(memory_space=pl.ANY),
            ],
            out_specs=pl.BlockSpec(
                (units, 1, 2 * QUAD, HEAD_WIDTH), lambda b, lengths: (0, b, 0, 0)
            ),
            scratch_shapes=[
                pltpu.VMEM((kv.shape[0] + halo.shape[0], kv.shape[1]), jnp.bfloat16),
                pltpu.VMEM((chunks, rows, 2 * BLOCK), jnp.float32),
                pltpu.VMEM((rows, BLOCK), jnp.float32),
                pltpu.VMEM((rows, BLOCK), jnp.float32),
                pltpu.VMEM((rows, HEAD_WIDTH), jnp.float32),
                pltpu.SemaphoreType.DMA((2,)),
            ],
        ),
        compiler_params=pltpu.CompilerParams(
            dimension_semantics=("arbitrary",), vmem_limit_bytes=32 << 20
        ),
        name="attend",
    )(lengths, q, kv, halo)


def route_kernel(index, x_ref, y_ref):
    def step(n, carry):
        for u in range(16):
            y_ref[n * 16 + u] = x_ref[index[n * 16 + u]]
        return carry

    lax.fori_loop(0, y_ref.shape[0] // 16, step, 0)


def route(index, x):
    return pl.pallas_call(
        route_kernel,
        out_shape=jax.ShapeDtypeStruct(x.shape, x.dtype),
        grid_spec=pltpu.PrefetchScalarGridSpec(
            num_scalar_prefetch=1,
            grid=(1,),
            in_specs=[pl.BlockSpec(x.shape, lambda i, index: (0, 0, 0))],
            out_specs=pl.BlockSpec(x.shape, lambda i, index: (0, 0, 0)),
        ),
        compiler_params=pltpu.CompilerParams(vmem_limit_bytes=32 << 20),
        name="route",
    )(index, x)


def on_device(queries, keys, values, doc_start, doc_blocks, doc_rank, doc_slot):
    ctx_count = lax.axis_size("ctx")
    head_count = lax.axis_size("head")
    rank_index = lax.axis_index("ctx")
    tokens = queries.shape[0]
    rows_per_rank = tokens * head_count
    blocks = rows_per_rank // BLOCK
    key_width = keys.shape[1] // head_count
    query_width = queries.shape[1] // head_count
    heads = query_width // HEAD_WIDTH

    kv = jnp.concatenate(
        [
            keys.reshape(tokens, head_count, key_width),
            values.reshape(tokens, head_count, key_width),
        ],
        axis=2,
    ).transpose(1, 0, 2)
    kv = lax.all_to_all(kv, "head", split_axis=0, concat_axis=0, tiled=True)
    kv = kv.reshape(rows_per_rank, 2 * key_width)
    halo = lax.ppermute(
        kv[BLOCK:], "ctx", [(i, (i + 1) % ctx_count) for i in range(ctx_count)]
    )
    q = queries.reshape(tokens, head_count, query_width).transpose(1, 0, 2)
    q = lax.all_to_all(q, "head", split_axis=0, concat_axis=0, tiled=True)
    q = q.reshape(rows_per_rank, query_width)

    own_blocks = rank_index * blocks + jnp.arange(blocks, dtype=jnp.int32)
    holds = (doc_start[None, :] <= own_blocks[:, None]) & (
        own_blocks[:, None] < (doc_start + doc_blocks)[None, :]
    )
    lengths = own_blocks + 1 - jnp.sum(jnp.where(holds, doc_start[None, :], 0), axis=1)

    new_blocks = jnp.arange(ctx_count * blocks, dtype=jnp.int32)
    first_new = doc_rank * blocks + doc_slot
    lands = (first_new[None, :] <= new_blocks[:, None]) & (
        new_blocks[:, None] < (first_new + doc_blocks)[None, :]
    )
    sources = new_blocks + jnp.sum(
        jnp.where(lands, (doc_start - first_new)[None, :], 0), axis=1
    )

    dealt = attend(lengths, q, kv, halo)
    dealt = lax.all_to_all(dealt, "ctx", split_axis=0, concat_axis=0, tiled=True)
    dealt = dealt.reshape(ctx_count * blocks, 2 * QUAD, HEAD_WIDTH)
    moved = route(sources, dealt)
    parts = tokens // HALF
    moved = moved.reshape(ctx_count * head_count, parts, QUAD, HEAD_WIDTH)
    placed = lax.all_to_all(moved, ("ctx", "head"), split_axis=0, concat_axis=0, tiled=True)
    placed = placed.reshape(HALF // QUAD, heads, head_count, parts, QUAD, HEAD_WIDTH)
    return placed.transpose(3, 0, 4, 2, 1, 5).reshape(tokens, queries.shape[1])


def solution(mesh):
    return jax.shard_map(
        on_device,
        mesh=mesh,
        in_specs=(
            P(("ctx", "head"), None),
            P(("ctx", "head"), None),
            P(("ctx", "head"), None),
            P(),
            P(),
            P(),
            P(),
        ),
        out_specs=P(("ctx", "head"), None),
        check_vma=False,
    )
```

```python
import functools
import math

import jax
import jax.numpy as jnp
from jax import lax
from jax.experimental import pallas as pl
from jax.experimental.pallas import tpu as pltpu
from jax.sharding import PartitionSpec as P

HEAD_WIDTH = 128
BLOCK = 128
HALF = 64
QUAD = 4
MASKED = -1e30
EXP2_SCALE = math.log2(math.e) / math.sqrt(HEAD_WIDTH)


def pack_kernel(*refs, pieces):
    out_hbm, sems = refs[-2:]
    copies = []
    for g in range(out_hbm.shape[0]):
        at = 0
        for n, (start, width) in enumerate(pieces):
            source = refs[n]
            first = g * (source.shape[1] // out_hbm.shape[0]) + start
            copies.append(
                pltpu.make_async_copy(
                    source.at[:, pl.ds(first, width)],
                    out_hbm.at[g, :, pl.ds(at, width)],
                    sems.at[n, g],
                )
            )
            at += width
    for copy in copies:
        copy.start()
    for copy in copies:
        copy.wait()


def pack(arrays, pieces, groups):
    tokens = arrays[0].shape[0]
    width = sum(width for _, width in pieces)
    return pl.pallas_call(
        functools.partial(pack_kernel, pieces=pieces),
        out_shape=jax.ShapeDtypeStruct((groups, tokens, width), arrays[0].dtype),
        in_specs=[pl.BlockSpec(memory_space=pl.ANY)] * len(arrays),
        out_specs=pl.BlockSpec(memory_space=pl.ANY),
        scratch_shapes=[pltpu.SemaphoreType.DMA((len(arrays), groups))],
        name="pack",
    )(*arrays)


def attend_block(lengths, q_ref, key_ref, turned_ref, out_ref, score_ref, acc_ref):
    block = pl.program_id(0)
    heads = q_ref.shape[1] // HEAD_WIDTH
    rows = heads * BLOCK
    length = lengths[block]
    chunks = (length + 1) // 2
    newest = key_ref.shape[0] // BLOCK - pl.num_programs(0) + block
    q = jnp.concatenate(
        [q_ref[:, h * HEAD_WIDTH : (h + 1) * HEAD_WIDTH] for h in range(heads)], axis=0
    )

    def scores_of(chunk):
        first = pl.multiple_of((newest - 1 - 2 * chunk) * BLOCK, BLOCK)
        keys = key_ref[pl.ds(first, 2 * BLOCK), :]
        s = lax.dot_general(keys, q, (((1,), (1,)), ((), ())), preferred_element_type=jnp.float32)
        return jnp.where(2 * chunk + 2 <= length, s[:BLOCK], MASKED), s[BLOCK:]

    def fold(x, op):
        return op(x.reshape(BLOCK // 8, 8, rows), axis=0)

    older, newer = scores_of(0)
    key_ids = lax.broadcasted_iota(jnp.int32, (BLOCK, rows), 0)
    query_ids = lax.broadcasted_iota(jnp.int32, (BLOCK, rows), 1) % BLOCK
    newer = jnp.where(key_ids <= query_ids, newer, MASKED)
    score_ref[0, :BLOCK] = older
    score_ref[0, BLOCK:] = newer

    def first_pass(chunk, top):
        older, newer = scores_of(chunk)
        score_ref[chunk, :BLOCK] = older
        score_ref[chunk, BLOCK:] = newer
        return jnp.maximum(top, fold(jnp.maximum(older, newer), jnp.max))

    top = lax.fori_loop(1, chunks, first_pass, fold(jnp.maximum(older, newer), jnp.max))
    shift = jnp.max(top, axis=0, keepdims=True) * EXP2_SCALE

    def weigh(chunk):
        weights = jnp.exp2(score_ref[chunk] * EXP2_SCALE - shift)
        total = fold(weights[:BLOCK] + weights[BLOCK:], jnp.sum)
        at = newest - 1 - 2 * chunk
        vals = jnp.concatenate([turned_ref[at], turned_ref[at + 1]], axis=1)
        out = jnp.dot(vals, weights.astype(jnp.bfloat16), preferred_element_type=jnp.float32)
        return total, out

    total, out = weigh(0)
    acc_ref[...] = out

    def second_pass(chunk, total):
        more, out = weigh(chunk)
        acc_ref[...] += out
        return total + more

    total = lax.fori_loop(1, chunks, second_pass, total)
    out = acc_ref[...] * (1.0 / jnp.sum(total, axis=0, keepdims=True))
    low = lax.broadcasted_iota(jnp.int32, (HALF, HEAD_WIDTH), 0) % (2 * QUAD) < QUAD
    quads = HALF // QUAD
    for h in range(heads):
        placed = out[:, h * BLOCK : (h + 1) * BLOCK].T
        upper = placed[:HALF]
        lower = placed[HALF:]
        even = jnp.where(low, upper, pltpu.roll(lower, QUAD, 0))
        odd = jnp.where(low, pltpu.roll(upper, HALF - QUAD, 0), lower)
        for k in range(quads // 2):
            tile = slice(2 * QUAD * k, 2 * QUAD * (k + 1))
            out_ref[h * quads + 2 * k, 0] = even[tile].astype(jnp.bfloat16)
            out_ref[h * quads + 2 * k + 1, 0] = odd[tile].astype(jnp.bfloat16)


def attend_first_kernel(
    lengths, q_ref, kv_hbm, halo_hbm, out_ref, turned_ref, key_ref, value_ref, score_ref, acc_ref, sems
):
    @pl.when(pl.program_id(0) == 0)
    def _():
        before = pl.ds(0, halo_hbm.shape[0])
        own = pl.ds(halo_hbm.shape[0], kv_hbm.shape[0])
        low = pl.ds(0, HEAD_WIDTH)
        high = pl.ds(HEAD_WIDTH, HEAD_WIDTH)
        copies = [
            pltpu.make_async_copy(kv_hbm.at[:, high], value_ref.at[own], sems.at[0]),
            pltpu.make_async_copy(halo_hbm.at[:, high], value_ref.at[before], sems.at[1]),
            pltpu.make_async_copy(kv_hbm.at[:, low], key_ref.at[own], sems.at[2]),
            pltpu.make_async_copy(halo_hbm.at[:, low], key_ref.at[before], sems.at[3]),
        ]
        for copy in copies:
            copy.start()
        for copy in copies:
            copy.wait()

        def turn(n, carry):
            first = pl.multiple_of(n * BLOCK, BLOCK)
            part = value_ref[pl.ds(first, BLOCK), :].astype(jnp.float32)
            turned_ref[n] = part.T.astype(jnp.bfloat16)
            return carry

        lax.fori_loop(0, turned_ref.shape[0], turn, 0)

    attend_block(lengths, q_ref, key_ref, turned_ref, out_ref, score_ref, acc_ref)


def attend_second_kernel(
    lengths,
    q_ref,
    kv_hbm,
    halo_hbm,
    turned_hbm,
    done_hbm,
    out_ref,
    key_ref,
    turned_ref,
    score_ref,
    acc_ref,
    sems,
):
    del done_hbm

    @pl.when(pl.program_id(0) == 0)
    def _():
        before = pl.ds(0, halo_hbm.shape[0])
        own = pl.ds(halo_hbm.shape[0], kv_hbm.shape[0])
        low = pl.ds(0, HEAD_WIDTH)
        copies = [
            pltpu.make_async_copy(kv_hbm.at[:, low], key_ref.at[own], sems.at[0]),
            pltpu.make_async_copy(halo_hbm.at[:, low], key_ref.at[before], sems.at[1]),
            pltpu.make_async_copy(turned_hbm, turned_ref, sems.at[2]),
        ]
        for copy in copies:
            copy.start()
        for copy in copies:
            copy.wait()

    attend_block(lengths, q_ref, key_ref, turned_ref, out_ref, score_ref, acc_ref)


def attend(lengths, q, kv, halo, earlier=None):
    blocks = q.shape[0] // BLOCK
    heads = q.shape[1] // HEAD_WIDTH
    units = HALF // QUAD * heads
    window = kv.shape[0] + halo.shape[0]
    rows = heads * BLOCK
    out_shape = jax.ShapeDtypeStruct((2 * units, blocks, 2 * QUAD, HEAD_WIDTH), jnp.bfloat16)
    turned_shape = (window // BLOCK, HEAD_WIDTH, BLOCK)
    hbm = pl.BlockSpec(memory_space=pl.ANY)
    turned_spec = pl.BlockSpec(turned_shape, lambda b, lengths: (0, 0, 0))
    specs = [pl.BlockSpec((BLOCK, q.shape[1]), lambda b, lengths: (b, 0)), hbm, hbm]
    part = 0 if earlier is None else 1
    out_spec = pl.BlockSpec(
        (units, 1, 2 * QUAD, HEAD_WIDTH), lambda b, lengths: (part, b, 0, 0)
    )
    keys = pltpu.VMEM((window, HEAD_WIDTH), jnp.bfloat16)
    work = [
        pltpu.VMEM(((blocks + 1) // 2, 2 * BLOCK, rows), jnp.float32),
        pltpu.VMEM((HEAD_WIDTH, rows), jnp.float32),
    ]
    params = pltpu.CompilerParams(
        dimension_semantics=("arbitrary",), vmem_limit_bytes=32 << 20
    )
    if earlier is None:
        return pl.pallas_call(
            attend_first_kernel,
            out_shape=(out_shape, jax.ShapeDtypeStruct(turned_shape, jnp.bfloat16)),
            grid_spec=pltpu.PrefetchScalarGridSpec(
                num_scalar_prefetch=1,
                grid=(blocks,),
                in_specs=specs,
                out_specs=(out_spec, turned_spec),
                scratch_shapes=[keys, keys] + work + [pltpu.SemaphoreType.DMA((4,))],
            ),
            compiler_params=params,
            name="attend_first",
        )(lengths, q, kv, halo)
    done, turned = earlier
    return pl.pallas_call(
        attend_second_kernel,
        out_shape=out_shape,
        grid_spec=pltpu.PrefetchScalarGridSpec(
            num_scalar_prefetch=1,
            grid=(blocks,),
            in_specs=specs + [hbm, hbm],
            out_specs=out_spec,
            scratch_shapes=[keys, pltpu.VMEM(turned_shape, jnp.bfloat16)]
            + work
            + [pltpu.SemaphoreType.DMA((3,))],
        ),
        input_output_aliases={5: 0},
        compiler_params=params,
        name="attend_second",
    )(lengths, q, kv, halo, turned, done)


def route_kernel(index, x_ref, y_ref):
    def step(n, carry):
        for u in range(16):
            y_ref[n * 16 + u] = x_ref[index[n * 16 + u]]
        return carry

    lax.fori_loop(0, y_ref.shape[0] // 16, step, 0)


def route(index, x):
    return pl.pallas_call(
        route_kernel,
        out_shape=jax.ShapeDtypeStruct(x.shape, x.dtype),
        grid_spec=pltpu.PrefetchScalarGridSpec(
            num_scalar_prefetch=1,
            grid=(1,),
            in_specs=[pl.BlockSpec(x.shape, lambda i, index: (0, 0, 0))],
            out_specs=pl.BlockSpec(x.shape, lambda i, index: (0, 0, 0)),
        ),
        compiler_params=pltpu.CompilerParams(vmem_limit_bytes=32 << 20),
        name="route",
    )(index, x)


def on_device(queries, keys, values, doc_start, doc_blocks, doc_rank, doc_slot):
    ctx_count = lax.axis_size("ctx")
    head_count = lax.axis_size("head")
    rank_index = lax.axis_index("ctx")
    tokens = queries.shape[0]
    rows_per_rank = tokens * head_count
    blocks = rows_per_rank // BLOCK
    key_width = keys.shape[1] // head_count
    query_width = queries.shape[1] // head_count
    heads = query_width // HEAD_WIDTH

    half_width = query_width // 2

    def gather_heads(x):
        x = lax.all_to_all(x, "head", split_axis=0, concat_axis=0, tiled=True)
        return x.reshape(rows_per_rank, x.shape[2])

    kv = gather_heads(pack((keys, values), ((0, key_width), (0, key_width)), head_count))
    halo = lax.ppermute(
        kv[BLOCK:], "ctx", [(i, (i + 1) % ctx_count) for i in range(ctx_count)]
    )
    q_first = gather_heads(pack((queries,), ((0, half_width),), head_count))
    packed = pack((queries,), ((half_width, half_width),), head_count)
    packed, q_first, halo = lax.optimization_barrier((packed, q_first, halo))
    q_second = gather_heads(packed)

    own_blocks = rank_index * blocks + jnp.arange(blocks, dtype=jnp.int32)
    holds = (doc_start[None, :] <= own_blocks[:, None]) & (
        own_blocks[:, None] < (doc_start + doc_blocks)[None, :]
    )
    lengths = own_blocks + 1 - jnp.sum(jnp.where(holds, doc_start[None, :], 0), axis=1)

    new_blocks = jnp.arange(ctx_count * blocks, dtype=jnp.int32)
    first_new = doc_rank * blocks + doc_slot
    lands = (first_new[None, :] <= new_blocks[:, None]) & (
        new_blocks[:, None] < (first_new + doc_blocks)[None, :]
    )
    sources = new_blocks + jnp.sum(
        jnp.where(lands, (doc_start - first_new)[None, :], 0), axis=1
    )

    dealt = attend(lengths, q_second, kv, halo, attend(lengths, q_first, kv, halo))
    dealt = lax.all_to_all(dealt, "ctx", split_axis=0, concat_axis=0, tiled=True)
    dealt = dealt.reshape(ctx_count * blocks, 2 * QUAD, HEAD_WIDTH)
    moved = route(sources, dealt)
    parts = tokens // HALF
    moved = moved.reshape(ctx_count * head_count, parts, QUAD, HEAD_WIDTH)
    placed = lax.all_to_all(moved, ("ctx", "head"), split_axis=0, concat_axis=0, tiled=True)
    placed = placed.reshape(heads, HALF // QUAD, head_count, parts, QUAD, HEAD_WIDTH)
    return placed.transpose(3, 1, 4, 2, 0, 5).reshape(tokens, queries.shape[1])


def solution(mesh):
    return jax.shard_map(
        on_device,
        mesh=mesh,
        in_specs=(
            P(("ctx", "head"), None),
            P(("ctx", "head"), None),
            P(("ctx", "head"), None),
            P(),
            P(),
            P(),
            P(),
        ),
        out_specs=P(("ctx", "head"), None),
        check_vma=False,
    )
```

```python
import functools
import math

import jax
import jax.numpy as jnp
from jax import lax
from jax.experimental import pallas as pl
from jax.experimental.pallas import tpu as pltpu
from jax.sharding import PartitionSpec as P

HEAD_WIDTH = 128
BLOCK = 128
HALF = 64
QUAD = 4
STEP = 4
MASKED = -1e30
EXP2_SCALE = math.log2(math.e) / math.sqrt(HEAD_WIDTH)


def pack_kernel(*refs, pieces):
    out_hbm, packed_ref, in_sems, out_sems = refs[-4:]
    groups = out_hbm.shape[0]
    loads = []
    stores = []
    for g in range(groups):
        at = 0
        for n, (start, width) in enumerate(pieces):
            source = refs[n]
            first = g * (source.shape[1] // groups) + start
            loads.append(
                pltpu.make_async_copy(
                    source.at[:, pl.ds(first, width)],
                    packed_ref.at[g, :, pl.ds(at, width)],
                    in_sems.at[g, n],
                )
            )
            at += width
        stores.append(pltpu.make_async_copy(packed_ref.at[g], out_hbm.at[g], out_sems.at[g]))
    for load in loads:
        load.start()
    for g in range(groups):
        for load in loads[g * len(pieces) : (g + 1) * len(pieces)]:
            load.wait()
        stores[g].start()
    for store in stores:
        store.wait()


def pack(arrays, pieces, groups):
    tokens = arrays[0].shape[0]
    shape = (groups, tokens, sum(width for _, width in pieces))
    return pl.pallas_call(
        functools.partial(pack_kernel, pieces=pieces),
        out_shape=jax.ShapeDtypeStruct(shape, arrays[0].dtype),
        in_specs=[pl.BlockSpec(memory_space=pl.ANY)] * len(arrays),
        out_specs=pl.BlockSpec(memory_space=pl.ANY),
        scratch_shapes=[
            pltpu.VMEM(shape, arrays[0].dtype),
            pltpu.SemaphoreType.DMA((groups, len(arrays))),
            pltpu.SemaphoreType.DMA((groups,)),
        ],
        name="pack",
    )(*arrays)


def attend_blocks(lengths, q_ref, key_ref, turned_ref, result_ref, out_hbm, part, sems):
    heads = q_ref.shape[1] // HEAD_WIDTH
    rows = heads * BLOCK
    blocks = result_ref.shape[0]
    units = result_ref.shape[1]
    before = key_ref.shape[0] // BLOCK - blocks
    quads = HALF // QUAD

    def store_of(block):
        return pltpu.make_async_copy(
            result_ref.at[block], out_hbm.at[pl.ds(part * units, units), block], sems.at[block]
        )

    def window(block, length, size):
        first = pl.multiple_of((before + block + 1 - size) * BLOCK, BLOCK)
        row = pl.multiple_of(block * BLOCK, BLOCK)
        q = jnp.concatenate(
            [
                q_ref[pl.ds(row, BLOCK), h * HEAD_WIDTH : (h + 1) * HEAD_WIDTH]
                for h in range(heads)
            ],
            axis=0,
        )
        keys = key_ref[pl.ds(first, size * BLOCK), :HEAD_WIDTH]
        s = lax.dot_general(keys, q, (((1,), (1,)), ((), ())), preferred_element_type=jnp.float32)
        pieces = [s[n * BLOCK : (n + 1) * BLOCK] for n in range(size)]
        for n in range(min(STEP, size) - 1):
            pieces[n] = jnp.where(size - n <= length, pieces[n], MASKED)
        key_ids = lax.broadcasted_iota(jnp.int32, (BLOCK, rows), 0)
        query_ids = lax.broadcasted_iota(jnp.int32, (BLOCK, rows), 1) % BLOCK
        pieces[-1] = jnp.where(key_ids <= query_ids, pieces[-1], MASKED)
        top = functools.reduce(jnp.maximum, pieces)
        shift = jnp.max(top, axis=0, keepdims=True) * EXP2_SCALE
        pieces = [jnp.exp2(piece * EXP2_SCALE - shift) for piece in pieces]
        total = jnp.sum(functools.reduce(jnp.add, pieces), axis=0, keepdims=True)
        weights = jnp.concatenate([piece.astype(jnp.bfloat16) for piece in pieces], axis=0)
        vals = jnp.concatenate(
            [turned_ref[before + block + 1 - size + n] for n in range(size)], axis=1
        )
        out = jnp.dot(vals, weights, preferred_element_type=jnp.float32) * (1.0 / total)
        low = lax.broadcasted_iota(jnp.int32, (HALF, HEAD_WIDTH), 0) % (2 * QUAD) < QUAD
        for h in range(heads):
            placed = out[:, h * BLOCK : (h + 1) * BLOCK].T
            upper = placed[:HALF]
            lower = placed[HALF:]
            even = jnp.where(low, upper, pltpu.roll(lower, QUAD, 0))
            odd = jnp.where(low, pltpu.roll(upper, HALF - QUAD, 0), lower)
            for k in range(quads // 2):
                tile = slice(2 * QUAD * k, 2 * QUAD * (k + 1))
                result_ref[block, h * quads + 2 * k] = even[tile].astype(jnp.bfloat16)
                result_ref[block, h * quads + 2 * k + 1] = odd[tile].astype(jnp.bfloat16)

    def step(block, carry):
        length = lengths[block]
        for size in range(STEP, blocks + STEP, STEP):

            @pl.when((length > size - STEP) & (length <= size))
            def _():
                window(block, length, min(size, before + 1))

        store_of(block).start()
        return carry

    lax.fori_loop(0, blocks, step, 0)
    for block in range(blocks):
        store_of(block).wait()


def attend_first_kernel(
    lengths,
    q_hbm,
    kv_hbm,
    halo_hbm,
    out_hbm,
    turned_hbm,
    q_ref,
    kv_ref,
    turned_ref,
    result_ref,
    in_sems,
    sems,
):
    before = halo_hbm.shape[0]
    copies = [
        pltpu.make_async_copy(q_hbm, q_ref, in_sems.at[0]),
        pltpu.make_async_copy(kv_hbm, kv_ref.at[pl.ds(before, kv_hbm.shape[0])], in_sems.at[1]),
        pltpu.make_async_copy(halo_hbm, kv_ref.at[pl.ds(0, before)], in_sems.at[2]),
    ]
    for copy in copies:
        copy.start()
    for copy in copies:
        copy.wait()

    def turn(n, carry):
        first = pl.multiple_of(n * BLOCK, BLOCK)
        part = kv_ref[pl.ds(first, BLOCK), HEAD_WIDTH:].astype(jnp.float32)
        turned_ref[n] = part.T.astype(jnp.bfloat16)
        return carry

    lax.fori_loop(0, turned_ref.shape[0], turn, 0)
    keep = pltpu.make_async_copy(turned_ref, turned_hbm, in_sems.at[3])
    keep.start()
    attend_blocks(lengths, q_ref, kv_ref, turned_ref, result_ref, out_hbm, 0, sems)
    keep.wait()


def attend_second_kernel(
    lengths,
    q_hbm,
    kv_hbm,
    halo_hbm,
    turned_hbm,
    done_hbm,
    out_hbm,
    q_ref,
    key_ref,
    turned_ref,
    result_ref,
    in_sems,
    sems,
):
    del done_hbm
    before = halo_hbm.shape[0]
    low = pl.ds(0, HEAD_WIDTH)
    own = pl.ds(before, kv_hbm.shape[0])
    copies = [
        pltpu.make_async_copy(q_hbm, q_ref, in_sems.at[0]),
        pltpu.make_async_copy(kv_hbm.at[:, low], key_ref.at[own], in_sems.at[1]),
        pltpu.make_async_copy(halo_hbm.at[:, low], key_ref.at[pl.ds(0, before)], in_sems.at[2]),
        pltpu.make_async_copy(turned_hbm, turned_ref, in_sems.at[3]),
    ]
    for copy in copies:
        copy.start()
    for copy in copies:
        copy.wait()
    attend_blocks(lengths, q_ref, key_ref, turned_ref, result_ref, out_hbm, 1, sems)


def attend(lengths, q, kv, halo, earlier=None):
    blocks = q.shape[0] // BLOCK
    units = HALF // QUAD * (q.shape[1] // HEAD_WIDTH)
    window = kv.shape[0] + halo.shape[0]
    out_shape = jax.ShapeDtypeStruct((2 * units, blocks, 2 * QUAD, HEAD_WIDTH), jnp.bfloat16)
    turned_shape = (window // BLOCK, HEAD_WIDTH, BLOCK)
    hbm = pl.BlockSpec(memory_space=pl.ANY)
    smem = pl.BlockSpec(memory_space=pltpu.SMEM)
    result = pltpu.VMEM((blocks, units, 2 * QUAD, HEAD_WIDTH), jnp.bfloat16)
    stores = pltpu.SemaphoreType.DMA((blocks,))
    params = pltpu.CompilerParams(vmem_limit_bytes=32 << 20)
    if earlier is None:
        return pl.pallas_call(
            attend_first_kernel,
            out_shape=(out_shape, jax.ShapeDtypeStruct(turned_shape, jnp.bfloat16)),
            in_specs=[smem, hbm, hbm, hbm],
            out_specs=(hbm, hbm),
            scratch_shapes=[
                pltpu.VMEM(q.shape, q.dtype),
                pltpu.VMEM((window, kv.shape[1]), kv.dtype),
                pltpu.VMEM(turned_shape, jnp.bfloat16),
                result,
                pltpu.SemaphoreType.DMA((4,)),
                stores,
            ],
            compiler_params=params,
            name="attend_first",
        )(lengths, q, kv, halo)
    done, turned = earlier
    return pl.pallas_call(
        attend_second_kernel,
        out_shape=out_shape,
        in_specs=[smem] + [hbm] * 5,
        out_specs=hbm,
        scratch_shapes=[
            pltpu.VMEM(q.shape, q.dtype),
            pltpu.VMEM((window, HEAD_WIDTH), kv.dtype),
            pltpu.VMEM(turned_shape, jnp.bfloat16),
            result,
            pltpu.SemaphoreType.DMA((4,)),
            stores,
        ],
        input_output_aliases={5: 0},
        compiler_params=params,
        name="attend_second",
    )(lengths, q, kv, halo, turned, done)


def route_kernel(index, x_ref, y_ref):
    def step(n, carry):
        for u in range(16):
            y_ref[n * 16 + u] = x_ref[index[n * 16 + u]]
        return carry

    lax.fori_loop(0, y_ref.shape[0] // 16, step, 0)


def route(index, x):
    return pl.pallas_call(
        route_kernel,
        out_shape=jax.ShapeDtypeStruct(x.shape, x.dtype),
        grid_spec=pltpu.PrefetchScalarGridSpec(
            num_scalar_prefetch=1,
            grid=(1,),
            in_specs=[pl.BlockSpec(x.shape, lambda i, index: (0, 0, 0))],
            out_specs=pl.BlockSpec(x.shape, lambda i, index: (0, 0, 0)),
        ),
        compiler_params=pltpu.CompilerParams(vmem_limit_bytes=32 << 20),
        name="route",
    )(index, x)


def on_device(queries, keys, values, doc_start, doc_blocks, doc_rank, doc_slot):
    ctx_count = lax.axis_size("ctx")
    head_count = lax.axis_size("head")
    rank_index = lax.axis_index("ctx")
    tokens = queries.shape[0]
    rows_per_rank = tokens * head_count
    blocks = rows_per_rank // BLOCK
    key_width = keys.shape[1] // head_count
    query_width = queries.shape[1] // head_count
    heads = query_width // HEAD_WIDTH

    half_width = query_width // 2

    def gather_heads(x):
        x = lax.all_to_all(x, "head", split_axis=0, concat_axis=0, tiled=True)
        return x.reshape(rows_per_rank, x.shape[2])

    kv = gather_heads(pack((keys, values), ((0, key_width), (0, key_width)), head_count))
    halo = lax.ppermute(
        kv[BLOCK:], "ctx", [(i, (i + 1) % ctx_count) for i in range(ctx_count)]
    )
    q_first = gather_heads(pack((queries,), ((0, half_width),), head_count))
    packed = pack((queries,), ((half_width, half_width),), head_count)
    packed, q_first, halo = lax.optimization_barrier((packed, q_first, halo))
    q_second = gather_heads(packed)

    own_blocks = rank_index * blocks + jnp.arange(blocks, dtype=jnp.int32)
    holds = (doc_start[None, :] <= own_blocks[:, None]) & (
        own_blocks[:, None] < (doc_start + doc_blocks)[None, :]
    )
    lengths = own_blocks + 1 - jnp.sum(jnp.where(holds, doc_start[None, :], 0), axis=1)

    new_blocks = jnp.arange(ctx_count * blocks, dtype=jnp.int32)
    first_new = doc_rank * blocks + doc_slot
    lands = (first_new[None, :] <= new_blocks[:, None]) & (
        new_blocks[:, None] < (first_new + doc_blocks)[None, :]
    )
    sources = new_blocks + jnp.sum(
        jnp.where(lands, (doc_start - first_new)[None, :], 0), axis=1
    )

    dealt = attend(lengths, q_second, kv, halo, attend(lengths, q_first, kv, halo))
    dealt = lax.all_to_all(dealt, "ctx", split_axis=0, concat_axis=0, tiled=True)
    dealt = dealt.reshape(ctx_count * blocks, 2 * QUAD, HEAD_WIDTH)
    moved = route(sources, dealt)
    parts = tokens // HALF
    moved = moved.reshape(ctx_count * head_count, parts, QUAD, HEAD_WIDTH)
    placed = lax.all_to_all(moved, ("ctx", "head"), split_axis=0, concat_axis=0, tiled=True)
    placed = placed.reshape(heads, HALF // QUAD, head_count, parts, QUAD, HEAD_WIDTH)
    return placed.transpose(3, 1, 4, 2, 0, 5).reshape(tokens, queries.shape[1])


def solution(mesh):
    return jax.shard_map(
        on_device,
        mesh=mesh,
        in_specs=(
            P(("ctx", "head"), None),
            P(("ctx", "head"), None),
            P(("ctx", "head"), None),
            P(),
            P(),
            P(),
            P(),
        ),
        out_specs=P(("ctx", "head"), None),
        check_vma=False,
    )
```

```python
import functools
import math

import jax
import jax.numpy as jnp
from jax import lax
from jax.experimental import pallas as pl
from jax.experimental.pallas import tpu as pltpu
from jax.sharding import PartitionSpec as P

HEAD_WIDTH = 128
BLOCK = 128
HALF = 64
QUAD = 4
STEP = 2
MASKED = -1e30
EXP2_SCALE = math.log2(math.e) / math.sqrt(HEAD_WIDTH)


def pack_kernel(*refs, pieces):
    out_hbm, packed_ref, in_sems, out_sems = refs[-4:]
    groups = out_hbm.shape[0]
    loads = []
    stores = []
    for g in range(groups):
        at = 0
        for n, (start, width) in enumerate(pieces):
            source = refs[n]
            first = g * (source.shape[1] // groups) + start
            loads.append(
                pltpu.make_async_copy(
                    source.at[:, pl.ds(first, width)],
                    packed_ref.at[g, :, pl.ds(at, width)],
                    in_sems.at[g, n],
                )
            )
            at += width
        stores.append(pltpu.make_async_copy(packed_ref.at[g], out_hbm.at[g], out_sems.at[g]))
    for load in loads:
        load.start()
    for g in range(groups):
        for load in loads[g * len(pieces) : (g + 1) * len(pieces)]:
            load.wait()
        stores[g].start()
    for store in stores:
        store.wait()


def pack(arrays, pieces, groups):
    tokens = arrays[0].shape[0]
    shape = (groups, tokens, sum(width for _, width in pieces))
    return pl.pallas_call(
        functools.partial(pack_kernel, pieces=pieces),
        out_shape=jax.ShapeDtypeStruct(shape, arrays[0].dtype),
        in_specs=[pl.BlockSpec(memory_space=pl.ANY)] * len(arrays),
        out_specs=pl.BlockSpec(memory_space=pl.ANY),
        scratch_shapes=[
            pltpu.VMEM(shape, arrays[0].dtype),
            pltpu.SemaphoreType.DMA((groups, len(arrays))),
            pltpu.SemaphoreType.DMA((groups,)),
        ],
        name="pack",
    )(*arrays)


def prepare_kernel(kv_ref, halo_ref, key_ref, turned_ref):
    before = halo_ref.shape[0]
    key_ref[:before] = halo_ref[:, :HEAD_WIDTH]
    key_ref[before:] = kv_ref[:, :HEAD_WIDTH]

    def turn_from(source_ref, at):
        def turn(n, carry):
            first = pl.multiple_of(n * BLOCK, BLOCK)
            part = source_ref[pl.ds(first, BLOCK), HEAD_WIDTH:].astype(jnp.float32)
            turned_ref[at + n] = part.T.astype(jnp.bfloat16)
            return carry

        lax.fori_loop(0, source_ref.shape[0] // BLOCK, turn, 0)

    turn_from(halo_ref, 0)
    turn_from(kv_ref, before // BLOCK)


def prepare(kv, halo):
    window = kv.shape[0] + halo.shape[0]
    vmem = pl.BlockSpec(memory_space=pltpu.VMEM)
    return pl.pallas_call(
        prepare_kernel,
        out_shape=(
            jax.ShapeDtypeStruct((window, HEAD_WIDTH), kv.dtype),
            jax.ShapeDtypeStruct((window // BLOCK, HEAD_WIDTH, BLOCK), kv.dtype),
        ),
        in_specs=[vmem, vmem],
        out_specs=(vmem, vmem),
        compiler_params=pltpu.CompilerParams(vmem_limit_bytes=8 << 20),
        name="prepare",
    )(kv, halo)


def attend_kernel(
    lengths, q_ref, key_ref, turned_ref, out_hbm, order_ref, acc_ref, result_ref, sems
):
    heads = q_ref.shape[1] // HEAD_WIDTH
    rows = heads * BLOCK
    blocks = q_ref.shape[0] // BLOCK
    before = key_ref.shape[0] // BLOCK - blocks
    quads = HALF // QUAD

    def store_of(block):
        return pltpu.make_async_copy(
            result_ref.at[block + 1], out_hbm.at[:, block], sems.at[block]
        )

    out_ids = lax.broadcasted_iota(jnp.int32, (BLOCK, BLOCK), 0)
    from_ids = out_ids // (2 * QUAD) * QUAD + out_ids % (2 * QUAD) // QUAD * HALF + out_ids % QUAD
    query_ids = lax.broadcasted_iota(jnp.int32, (BLOCK, BLOCK), 1)
    order_ref[...] = (from_ids == query_ids).astype(jnp.bfloat16)

    def finish(slot):
        order = order_ref[...]
        for h in range(heads):
            placed = lax.dot_general(
                order,
                acc_ref[:, h * BLOCK : (h + 1) * BLOCK],
                (((1,), (1,)), ((), ())),
                preferred_element_type=jnp.float32,
            )
            result_ref[slot, h * quads : (h + 1) * quads] = placed.reshape(
                quads, 2 * QUAD, HEAD_WIDTH
            ).astype(jnp.bfloat16)

    def window(block, length, size):
        finish(block)
        first = pl.multiple_of((before + block + 1 - size) * BLOCK, BLOCK)
        row = pl.multiple_of(block * BLOCK, BLOCK)
        q = jnp.concatenate(
            [
                q_ref[pl.ds(row, BLOCK), h * HEAD_WIDTH : (h + 1) * HEAD_WIDTH]
                for h in range(heads)
            ],
            axis=0,
        )
        keys = key_ref[pl.ds(first, size * BLOCK), :]
        s = lax.dot_general(keys, q, (((1,), (1,)), ((), ())), preferred_element_type=jnp.float32)
        pieces = [s[n * BLOCK : (n + 1) * BLOCK] for n in range(size)]
        for n in range(min(STEP, size) - 1):
            pieces[n] = jnp.where(size - n <= length, pieces[n], MASKED)
        key_ids = lax.broadcasted_iota(jnp.int32, (BLOCK, rows), 0)
        query_ids = lax.broadcasted_iota(jnp.int32, (BLOCK, rows), 1) % BLOCK
        pieces[-1] = jnp.where(key_ids <= query_ids, pieces[-1], MASKED)
        top = functools.reduce(jnp.maximum, pieces)
        shift = jnp.max(top, axis=0, keepdims=True) * EXP2_SCALE
        pieces = [jnp.exp2(piece * EXP2_SCALE - shift) for piece in pieces]
        total = jnp.sum(functools.reduce(jnp.add, pieces), axis=0, keepdims=True)
        weights = jnp.concatenate([piece.astype(jnp.bfloat16) for piece in pieces], axis=0)
        vals = jnp.concatenate(
            [turned_ref[before + block + 1 - size + n] for n in range(size)], axis=1
        )
        out = jnp.dot(vals, weights, preferred_element_type=jnp.float32)
        acc_ref[...] = (out * (1.0 / total)).astype(jnp.bfloat16)

    def step(block, carry):
        length = lengths[block]
        for size in range(STEP, blocks + STEP, STEP):

            @pl.when((length > size - STEP) & (length <= size))
            def _():
                window(block, length, min(size, before + 1))

        @pl.when(block > 0)
        def _():
            store_of(block - 1).start()

        return carry

    lax.fori_loop(0, blocks, step, 0)
    finish(blocks)
    store_of(blocks - 1).start()
    for block in range(blocks):
        store_of(block).wait()


def attend(lengths, q, keys, turned):
    blocks = q.shape[0] // BLOCK
    heads = q.shape[1] // HEAD_WIDTH
    units = HALF // QUAD * heads
    vmem = pl.BlockSpec(memory_space=pltpu.VMEM)
    tile = (2 * QUAD, HEAD_WIDTH)
    return pl.pallas_call(
        attend_kernel,
        out_shape=jax.ShapeDtypeStruct((units, blocks) + tile, jnp.bfloat16),
        in_specs=[pl.BlockSpec(memory_space=pltpu.SMEM), vmem, vmem, vmem],
        out_specs=pl.BlockSpec(memory_space=pl.ANY),
        scratch_shapes=[
            pltpu.VMEM((BLOCK, BLOCK), jnp.bfloat16),
            pltpu.VMEM((HEAD_WIDTH, heads * BLOCK), jnp.bfloat16),
            pltpu.VMEM((blocks + 1, units) + tile, jnp.bfloat16),
            pltpu.SemaphoreType.DMA((blocks,)),
        ],
        compiler_params=pltpu.CompilerParams(vmem_limit_bytes=20 << 20),
        name="attend",
    )(lengths, q, keys, turned)


def route_kernel(index, x_ref, y_ref):
    def step(n, carry):
        for u in range(16):
            y_ref[n * 16 + u] = x_ref[index[n * 16 + u]]
        return carry

    lax.fori_loop(0, y_ref.shape[0] // 16, step, 0)


def route(index, x):
    vmem = pl.BlockSpec(memory_space=pltpu.VMEM)
    return pl.pallas_call(
        route_kernel,
        out_shape=jax.ShapeDtypeStruct(x.shape, x.dtype),
        in_specs=[pl.BlockSpec(memory_space=pltpu.SMEM), vmem],
        out_specs=vmem,
        compiler_params=pltpu.CompilerParams(vmem_limit_bytes=8 << 20),
        name="route",
    )(index, x)


def settle_kernel(x_ref, y_ref):
    heads, quads, groups, parts = x_ref.shape[:4]

    def step(n, carry):
        half = n % 2
        pair = n // 2
        for p in range(parts):
            for g in range(groups):
                for h in range(heads):
                    y_ref[p * (quads // 2) + pair, g * heads + h, half] = x_ref[h, n, g, p]
        return carry

    lax.fori_loop(0, quads, step, 0)


def settle(x):
    heads, quads, groups, parts = x.shape[:4]
    vmem = pl.BlockSpec(memory_space=pltpu.VMEM)
    return pl.pallas_call(
        settle_kernel,
        out_shape=jax.ShapeDtypeStruct(
            (parts * quads // 2, groups * heads, 2) + x.shape[4:], x.dtype
        ),
        in_specs=[vmem],
        out_specs=vmem,
        compiler_params=pltpu.CompilerParams(vmem_limit_bytes=8 << 20),
        name="settle",
    )(x)


def on_device(queries, keys, values, doc_start, doc_blocks, doc_rank, doc_slot):
    ctx_count = lax.axis_size("ctx")
    head_count = lax.axis_size("head")
    rank_index = lax.axis_index("ctx")
    tokens = queries.shape[0]
    rows_per_rank = tokens * head_count
    blocks = rows_per_rank // BLOCK
    key_width = keys.shape[1] // head_count
    query_width = queries.shape[1] // head_count
    heads = query_width // HEAD_WIDTH


    def gather_heads(x):
        x = lax.all_to_all(x, "head", split_axis=0, concat_axis=0, tiled=True)
        return x.reshape(rows_per_rank, x.shape[2])

    kv = gather_heads(pack((keys, values), ((0, key_width), (0, key_width)), head_count))
    halo = lax.ppermute(
        kv[BLOCK:], "ctx", [(i, (i + 1) % ctx_count) for i in range(ctx_count)]
    )
    keys, turned = prepare(kv, halo)
    q = gather_heads(pack((queries,), ((0, query_width),), head_count))

    own_blocks = rank_index * blocks + jnp.arange(blocks, dtype=jnp.int32)
    holds = (doc_start[None, :] <= own_blocks[:, None]) & (
        own_blocks[:, None] < (doc_start + doc_blocks)[None, :]
    )
    lengths = own_blocks + 1 - jnp.sum(jnp.where(holds, doc_start[None, :], 0), axis=1)

    new_blocks = jnp.arange(ctx_count * blocks, dtype=jnp.int32)
    first_new = doc_rank * blocks + doc_slot
    lands = (first_new[None, :] <= new_blocks[:, None]) & (
        new_blocks[:, None] < (first_new + doc_blocks)[None, :]
    )
    sources = new_blocks + jnp.sum(
        jnp.where(lands, (doc_start - first_new)[None, :], 0), axis=1
    )

    dealt = attend(lengths, q, keys, turned)
    dealt = lax.all_to_all(dealt, "ctx", split_axis=0, concat_axis=0, tiled=True)
    dealt = dealt.reshape(ctx_count * blocks, 2 * QUAD, HEAD_WIDTH)
    moved = route(sources, dealt)
    parts = tokens // HALF
    moved = moved.reshape(ctx_count * head_count, parts, QUAD, HEAD_WIDTH)
    placed = lax.all_to_all(moved, ("ctx", "head"), split_axis=0, concat_axis=0, tiled=True)
    placed = placed.reshape(heads, HALF // QUAD, head_count, parts, QUAD, HEAD_WIDTH)
    settled = settle(placed)
    settled = settled.reshape(settled.shape[:2] + (2 * QUAD, HEAD_WIDTH))
    return settled.transpose(0, 2, 1, 3).reshape(tokens, queries.shape[1])


def solution(mesh):
    return jax.shard_map(
        on_device,
        mesh=mesh,
        in_specs=(
            P(("ctx", "head"), None),
            P(("ctx", "head"), None),
            P(("ctx", "head"), None),
            P(),
            P(),
            P(),
            P(),
        ),
        out_specs=P(("ctx", "head"), None),
        check_vma=False,
    )
```

```python
import functools
import math

import jax
import jax.numpy as jnp
from jax import lax
from jax.experimental import pallas as pl
from jax.experimental.pallas import tpu as pltpu
from jax.sharding import PartitionSpec as P

HEAD_WIDTH = 128
BLOCK = 128
HALF = 64
QUAD = 4
STEP = 2
MASKED = -1e30
EXP2_SCALE = math.log2(math.e) / math.sqrt(HEAD_WIDTH)


def pack_kernel(*refs, pieces):
    out_hbm, packed_ref, in_sems, out_sems = refs[-4:]
    groups = out_hbm.shape[0]
    loads = []
    stores = []
    for g in range(groups):
        at = 0
        for n, (start, width) in enumerate(pieces):
            source = refs[n]
            first = g * (source.shape[1] // groups) + start
            loads.append(
                pltpu.make_async_copy(
                    source.at[:, pl.ds(first, width)],
                    packed_ref.at[g, :, pl.ds(at, width)],
                    in_sems.at[g, n],
                )
            )
            at += width
        stores.append(pltpu.make_async_copy(packed_ref.at[g], out_hbm.at[g], out_sems.at[g]))
    for load in loads:
        load.start()
    for g in range(groups):
        for load in loads[g * len(pieces) : (g + 1) * len(pieces)]:
            load.wait()
        stores[g].start()
    for store in stores:
        store.wait()


def pack(arrays, pieces, groups):
    tokens = arrays[0].shape[0]
    shape = (groups, tokens, sum(width for _, width in pieces))
    return pl.pallas_call(
        functools.partial(pack_kernel, pieces=pieces),
        out_shape=jax.ShapeDtypeStruct(shape, arrays[0].dtype),
        in_specs=[pl.BlockSpec(memory_space=pl.ANY)] * len(arrays),
        out_specs=pl.BlockSpec(memory_space=pl.ANY),
        scratch_shapes=[
            pltpu.VMEM(shape, arrays[0].dtype),
            pltpu.SemaphoreType.DMA((groups, len(arrays))),
            pltpu.SemaphoreType.DMA((groups,)),
        ],
        name="pack",
    )(*arrays)


def pack_turns_kernel(at, source, *refs):
    outs = refs[:-3]
    packed_ref, in_sems, out_sems = refs[-3:]
    groups = len(outs)
    width = packed_ref.shape[2]
    pitch = source.shape[1] // groups
    loads = []
    stores = []
    for k in range(groups):
        group = lax.rem(at[0] + k, groups)
        first = pl.multiple_of(group * pitch + (pitch - width), HEAD_WIDTH)
        loads.append(
            pltpu.make_async_copy(
                source.at[:, pl.ds(first, width)], packed_ref.at[k], in_sems.at[k]
            )
        )
        stores.append(pltpu.make_async_copy(packed_ref.at[k], outs[k], out_sems.at[k]))
    for load in loads:
        load.start()
    for load, store in zip(loads, stores):
        load.wait()
        store.start()
    for store in stores:
        store.wait()


def pack_turns(at, array, width, groups):
    shape = (array.shape[0], width)
    hbm = pl.BlockSpec(memory_space=pl.ANY)
    return pl.pallas_call(
        pack_turns_kernel,
        out_shape=(jax.ShapeDtypeStruct(shape, array.dtype),) * groups,
        in_specs=[pl.BlockSpec(memory_space=pltpu.SMEM), hbm],
        out_specs=(hbm,) * groups,
        scratch_shapes=[
            pltpu.VMEM((groups,) + shape, array.dtype),
            pltpu.SemaphoreType.DMA((groups,)),
            pltpu.SemaphoreType.DMA((groups,)),
        ],
        name="pack_turns",
    )(at, array)


def join_kernel(at, *refs):
    pieces = refs[:-1]
    out_ref = refs[-1]
    groups = len(pieces)
    rows = pieces[0].shape[0]
    for k in range(groups):
        first = pl.multiple_of(lax.rem(at[0] + groups - k, groups) * rows, HALF)
        out_ref[pl.ds(first, rows), :] = pieces[k][...]


def join(at, pieces):
    rows, width = pieces[0].shape
    vmem = pl.BlockSpec(memory_space=pltpu.VMEM)
    return pl.pallas_call(
        join_kernel,
        out_shape=jax.ShapeDtypeStruct((rows * len(pieces), width), pieces[0].dtype),
        in_specs=[pl.BlockSpec(memory_space=pltpu.SMEM)] + [vmem] * len(pieces),
        out_specs=vmem,
        compiler_params=pltpu.CompilerParams(vmem_limit_bytes=8 << 20),
        name="join",
    )(at, *pieces)


def prepare_kernel(kv_ref, halo_ref, key_ref, turned_ref):
    before = halo_ref.shape[0]
    key_ref[:before] = halo_ref[:, :HEAD_WIDTH]
    key_ref[before:] = kv_ref[:, :HEAD_WIDTH]

    def turn_from(source_ref, at):
        def turn(n, carry):
            first = pl.multiple_of(n * BLOCK, BLOCK)
            part = source_ref[pl.ds(first, BLOCK), HEAD_WIDTH:].astype(jnp.float32)
            turned_ref[at + n] = part.T.astype(jnp.bfloat16)
            return carry

        lax.fori_loop(0, source_ref.shape[0] // BLOCK, turn, 0)

    turn_from(halo_ref, 0)
    turn_from(kv_ref, before // BLOCK)


def prepare(kv, halo):
    window = kv.shape[0] + halo.shape[0]
    vmem = pl.BlockSpec(memory_space=pltpu.VMEM)
    return pl.pallas_call(
        prepare_kernel,
        out_shape=(
            jax.ShapeDtypeStruct((window, HEAD_WIDTH), kv.dtype),
            jax.ShapeDtypeStruct((window // BLOCK, HEAD_WIDTH, BLOCK), kv.dtype),
        ),
        in_specs=[vmem, vmem],
        out_specs=(vmem, vmem),
        compiler_params=pltpu.CompilerParams(vmem_limit_bytes=8 << 20),
        name="prepare",
    )(kv, halo)


def attend_kernel(
    lengths, q_ref, key_ref, turned_ref, out_hbm, order_ref, acc_ref, result_ref, sems, *, flip
):
    heads = q_ref.shape[1] // HEAD_WIDTH
    rows = heads * BLOCK
    blocks = q_ref.shape[0] // BLOCK
    before = key_ref.shape[0] // BLOCK - blocks
    quads = HALF // QUAD

    def store_of(block):
        return pltpu.make_async_copy(
            result_ref.at[block + 1], out_hbm.at[:, block], sems.at[block]
        )

    out_ids = lax.broadcasted_iota(jnp.int32, (2 * BLOCK, BLOCK), 0)
    from_ids = out_ids // (2 * QUAD) * QUAD + out_ids % QUAD
    query_ids = lax.broadcasted_iota(jnp.int32, (2 * BLOCK, BLOCK), 1)
    order_ref[...] = (from_ids == query_ids).astype(jnp.bfloat16)

    def finish(slot):
        order = order_ref[...]
        for h in range(heads):
            placed = lax.dot_general(
                order,
                acc_ref[:, h * BLOCK : (h + 1) * BLOCK],
                (((1,), (1,)), ((), ())),
                preferred_element_type=jnp.float32,
            )
            placed = placed.reshape(2 * quads, 2 * QUAD, HEAD_WIDTH)[:, :QUAD].astype(jnp.bfloat16)
            for half in range(2):
                first = ((half + flip) % 2 * heads + h) * quads
                result_ref[slot, first : first + quads] = placed[half * quads : (half + 1) * quads]

    def window(block, length, size):
        finish(block)
        first = pl.multiple_of((before + block + 1 - size) * BLOCK, BLOCK)
        row = pl.multiple_of(block * BLOCK, BLOCK)
        q = jnp.concatenate(
            [
                q_ref[pl.ds(row, BLOCK), h * HEAD_WIDTH : (h + 1) * HEAD_WIDTH]
                for h in range(heads)
            ],
            axis=0,
        )
        keys = key_ref[pl.ds(first, size * BLOCK), :]
        s = lax.dot_general(keys, q, (((1,), (1,)), ((), ())), preferred_element_type=jnp.float32)
        pieces = [s[n * BLOCK : (n + 1) * BLOCK] for n in range(size)]
        for n in range(min(STEP, size) - 1):
            pieces[n] = jnp.where(size - n <= length, pieces[n], MASKED)
        key_ids = lax.broadcasted_iota(jnp.int32, (BLOCK, rows), 0)
        query_ids = lax.broadcasted_iota(jnp.int32, (BLOCK, rows), 1) % BLOCK
        pieces[-1] = jnp.where(key_ids <= query_ids, pieces[-1], MASKED)
        top = functools.reduce(jnp.maximum, pieces)
        shift = jnp.max(top, axis=0, keepdims=True) * EXP2_SCALE
        pieces = [jnp.exp2(piece * EXP2_SCALE - shift) for piece in pieces]
        total = jnp.sum(functools.reduce(jnp.add, pieces), axis=0, keepdims=True)
        weights = jnp.concatenate([piece.astype(jnp.bfloat16) for piece in pieces], axis=0)
        vals = jnp.concatenate(
            [turned_ref[before + block + 1 - size + n] for n in range(size)], axis=1
        )
        out = jnp.dot(vals, weights, preferred_element_type=jnp.float32)
        acc_ref[...] = (out * (1.0 / total)).astype(jnp.bfloat16)

    def step(block, carry):
        length = lengths[block]
        for size in range(STEP, blocks + STEP, STEP):

            @pl.when((length > size - STEP) & (length <= size))
            def _():
                window(block, length, min(size, before + 1))

        @pl.when(block > 0)
        def _():
            store_of(block - 1).start()

        return carry

    lax.fori_loop(0, blocks, step, 0)
    finish(blocks)
    store_of(blocks - 1).start()
    for block in range(blocks):
        store_of(block).wait()


def attend(lengths, q, keys, turned, flip):
    blocks = q.shape[0] // BLOCK
    heads = q.shape[1] // HEAD_WIDTH
    units = BLOCK // QUAD * heads
    vmem = pl.BlockSpec(memory_space=pltpu.VMEM)
    tile = (QUAD, HEAD_WIDTH)
    return pl.pallas_call(
        functools.partial(attend_kernel, flip=flip),
        out_shape=jax.ShapeDtypeStruct((units, blocks) + tile, jnp.bfloat16),
        in_specs=[pl.BlockSpec(memory_space=pltpu.SMEM), vmem, vmem, vmem],
        out_specs=pl.BlockSpec(memory_space=pl.ANY),
        scratch_shapes=[
            pltpu.VMEM((2 * BLOCK, BLOCK), jnp.bfloat16),
            pltpu.VMEM((HEAD_WIDTH, heads * BLOCK), jnp.bfloat16),
            pltpu.VMEM((blocks + 1, units) + tile, jnp.bfloat16),
            pltpu.SemaphoreType.DMA((blocks,)),
        ],
        compiler_params=pltpu.CompilerParams(vmem_limit_bytes=20 << 20),
        name="attend",
    )(lengths, q, keys, turned)


def route_kernel(index, upper_half, first_ref, second_ref, y_ref):
    def copy_from(refs):
        def step(n, carry):
            for u in range(8):
                block = n * 8 + u
                source = index[block]
                y_ref[2 * block] = refs[0][source]
                y_ref[2 * block + 1] = refs[1][source]
            return carry

        lax.fori_loop(0, first_ref.shape[0] // 8, step, 0)

    @pl.when(upper_half[0] == 0)
    def _():
        copy_from((first_ref, second_ref))

    @pl.when(upper_half[0] != 0)
    def _():
        copy_from((second_ref, first_ref))


def route(index, upper_half, first, second):
    vmem = pl.BlockSpec(memory_space=pltpu.VMEM)
    smem = pl.BlockSpec(memory_space=pltpu.SMEM)
    return pl.pallas_call(
        route_kernel,
        out_shape=jax.ShapeDtypeStruct((2 * first.shape[0],) + first.shape[1:], first.dtype),
        in_specs=[smem, smem, vmem, vmem],
        out_specs=vmem,
        compiler_params=pltpu.CompilerParams(vmem_limit_bytes=8 << 20),
        name="route",
    )(index, upper_half, first, second)


def settle_kernel(at, x_ref, y_ref):
    swaps, heads, quads, groups, parts = x_ref.shape[:5]

    def step(n, carry):
        half = n % 2
        pair = n // 2
        for p in range(parts):
            odd = (at[0] + p) % 2
            for c in range(swaps):
                side = lax.rem(odd + c, swaps)
                for g in range(groups):
                    for h in range(heads):
                        lane = (g * swaps + c) * heads + h
                        y_ref[p * (quads // 2) + pair, lane, half] = x_ref[side, h, n, g, p]
        return carry

    lax.fori_loop(0, quads, step, 0)


def settle(at, x):
    swaps, heads, quads, groups, parts = x.shape[:5]
    vmem = pl.BlockSpec(memory_space=pltpu.VMEM)
    return pl.pallas_call(
        settle_kernel,
        out_shape=jax.ShapeDtypeStruct(
            (parts * quads // 2, groups * swaps * heads, 2) + x.shape[5:], x.dtype
        ),
        in_specs=[pl.BlockSpec(memory_space=pltpu.SMEM), vmem],
        out_specs=vmem,
        compiler_params=pltpu.CompilerParams(vmem_limit_bytes=8 << 20),
        name="settle",
    )(at, x)


def on_device(queries, keys, values, doc_start, doc_blocks, doc_rank, doc_slot):
    ctx_count = lax.axis_size("ctx")
    head_count = lax.axis_size("head")
    rank_index = lax.axis_index("ctx")
    tokens = queries.shape[0]
    rows_per_rank = tokens * head_count
    blocks = rows_per_rank // BLOCK
    key_width = keys.shape[1] // head_count
    query_width = queries.shape[1] // head_count
    heads = query_width // HEAD_WIDTH


    def gather_heads(x):
        x = lax.all_to_all(x, "head", split_axis=0, concat_axis=0, tiled=True)
        return x.reshape(rows_per_rank, x.shape[2])

    kv = gather_heads(pack((keys, values), ((0, key_width), (0, key_width)), head_count))
    halo = lax.ppermute(
        kv[BLOCK:], "ctx", [(i, (i + 1) % ctx_count) for i in range(ctx_count)]
    )
    keys, turned = prepare(kv, halo)
    half_width = query_width // 2
    place = jnp.reshape(lax.axis_index("head"), (1,))
    q_first = gather_heads(pack((queries,), ((0, half_width),), head_count))
    pieces = pack_turns(place, queries, half_width, head_count)

    own_blocks = rank_index * blocks + jnp.arange(blocks, dtype=jnp.int32)
    holds = (doc_start[None, :] <= own_blocks[:, None]) & (
        own_blocks[:, None] < (doc_start + doc_blocks)[None, :]
    )
    lengths = own_blocks + 1 - jnp.sum(jnp.where(holds, doc_start[None, :], 0), axis=1)

    new_blocks = jnp.arange(ctx_count * blocks, dtype=jnp.int32)
    first_new = doc_rank * blocks + doc_slot
    lands = (first_new[None, :] <= new_blocks[:, None]) & (
        new_blocks[:, None] < (first_new + doc_blocks)[None, :]
    )
    sources = new_blocks + jnp.sum(
        jnp.where(lands, (doc_start - first_new)[None, :], 0), axis=1
    )

    def deal(x):
        x = lax.all_to_all(x, "ctx", split_axis=0, concat_axis=0, tiled=True)
        return x.reshape(ctx_count * blocks, QUAD, HEAD_WIDTH)

    done = attend(lengths, q_first, keys, turned, 0)
    done, *pieces = lax.optimization_barrier((done, *pieces))
    first = deal(done)
    pieces = [pieces[0]] + [
        lax.ppermute(
            pieces[k], "head", [(i, (i + k) % head_count) for i in range(head_count)]
        )
        for k in range(1, head_count)
    ]
    second = deal(attend(lengths, join(place, pieces), keys, turned, 1))
    upper_half = jnp.reshape(rank_index // (ctx_count // 2), (1,))
    moved = route(sources, upper_half, first, second)
    parts = tokens // HALF
    moved = moved.reshape(ctx_count * head_count, parts, QUAD, HEAD_WIDTH)
    placed = lax.all_to_all(moved, ("ctx", "head"), split_axis=0, concat_axis=0, tiled=True)
    placed = placed.reshape(2, heads // 2, HALF // QUAD, head_count, parts, QUAD, HEAD_WIDTH)
    settled = settle(place, placed)
    settled = settled.reshape(settled.shape[:2] + (2 * QUAD, HEAD_WIDTH))
    return settled.transpose(0, 2, 1, 3).reshape(tokens, queries.shape[1])


def solution(mesh):
    return jax.shard_map(
        on_device,
        mesh=mesh,
        in_specs=(
            P(("ctx", "head"), None),
            P(("ctx", "head"), None),
            P(("ctx", "head"), None),
            P(),
            P(),
            P(),
            P(),
        ),
        out_specs=P(("ctx", "head"), None),
        check_vma=False,
    )
```

```python
import functools
import math

import jax
import jax.numpy as jnp
from jax import lax
from jax.experimental import pallas as pl
from jax.experimental.pallas import tpu as pltpu
from jax.sharding import PartitionSpec as P

HEAD_WIDTH = 128
BLOCK = 128
HALF = 64
QUAD = 4
STEP = 4
MASKED = -1e30
EXP2_SCALE = math.log2(math.e) / math.sqrt(HEAD_WIDTH)


def pack_kernel(*refs, pieces):
    out_hbm, packed_ref, in_sems, out_sems = refs[-4:]
    groups = out_hbm.shape[0]
    loads = []
    stores = []
    for g in range(groups):
        at = 0
        for n, (start, width) in enumerate(pieces):
            source = refs[n]
            first = g * (source.shape[1] // groups) + start
            loads.append(
                pltpu.make_async_copy(
                    source.at[:, pl.ds(first, width)],
                    packed_ref.at[g, :, pl.ds(at, width)],
                    in_sems.at[g, n],
                )
            )
            at += width
        stores.append(pltpu.make_async_copy(packed_ref.at[g], out_hbm.at[g], out_sems.at[g]))
    for load in loads:
        load.start()
    for g in range(groups):
        for load in loads[g * len(pieces) : (g + 1) * len(pieces)]:
            load.wait()
        stores[g].start()
    for store in stores:
        store.wait()


def pack(arrays, pieces, groups):
    tokens = arrays[0].shape[0]
    shape = (groups, tokens, sum(width for _, width in pieces))
    return pl.pallas_call(
        functools.partial(pack_kernel, pieces=pieces),
        out_shape=jax.ShapeDtypeStruct(shape, arrays[0].dtype),
        in_specs=[pl.BlockSpec(memory_space=pl.ANY)] * len(arrays),
        out_specs=pl.BlockSpec(memory_space=pl.ANY),
        scratch_shapes=[
            pltpu.VMEM(shape, arrays[0].dtype),
            pltpu.SemaphoreType.DMA((groups, len(arrays))),
            pltpu.SemaphoreType.DMA((groups,)),
        ],
        name="pack",
    )(*arrays)


def prepare_kernel(kv_ref, halo_hbm, key_ref, turned_ref, halo_ref, sem):
    before = halo_ref.shape[0]
    load = pltpu.make_async_copy(halo_hbm, halo_ref, sem)
    load.start()

    def place(source_ref, at):
        key_ref[pl.ds(at, source_ref.shape[0]), :] = source_ref[:, :HEAD_WIDTH]

        def turn(n, carry):
            first = pl.multiple_of(n * BLOCK, BLOCK)
            part = source_ref[pl.ds(first, BLOCK), HEAD_WIDTH : 2 * HEAD_WIDTH].astype(jnp.float32)
            turned_ref[at // BLOCK + n] = part.T.astype(jnp.bfloat16)
            return carry

        lax.fori_loop(0, source_ref.shape[0] // BLOCK, turn, 0)

    place(kv_ref, before)
    load.wait()
    place(halo_ref, 0)


def prepare(kv, halo):
    window = kv.shape[0] + halo.shape[0]
    vmem = pl.BlockSpec(memory_space=pltpu.VMEM)
    return pl.pallas_call(
        prepare_kernel,
        out_shape=(
            jax.ShapeDtypeStruct((window, HEAD_WIDTH), kv.dtype),
            jax.ShapeDtypeStruct((window // BLOCK, HEAD_WIDTH, BLOCK), kv.dtype),
        ),
        in_specs=[vmem, pl.BlockSpec(memory_space=pl.ANY)],
        out_specs=(vmem, vmem),
        scratch_shapes=[pltpu.VMEM(halo.shape, halo.dtype), pltpu.SemaphoreType.DMA(())],
        compiler_params=pltpu.CompilerParams(vmem_limit_bytes=8 << 20),
        name="prepare",
    )(kv, halo)


def attend_kernel(lengths, q_ref, key_ref, turned_hbm, *refs, first_lane, part):
    out_hbm, turned_ref, order_ref, score_ref, top_ref, acc_ref, result_ref, load_sem, sems = refs[-9:]
    load = pltpu.make_async_copy(turned_hbm, turned_ref, load_sem)
    load.start()
    units = result_ref.shape[1]
    quads = HALF // QUAD
    heads = units // quads
    rows = heads * BLOCK
    blocks = q_ref.shape[0] // BLOCK
    before = key_ref.shape[0] // BLOCK - blocks

    def fold(x, op):
        return op(x.reshape(BLOCK // 8, 8, rows), axis=0)

    def store_of(block):
        return pltpu.make_async_copy(
            result_ref.at[block + 1], out_hbm.at[pl.ds(part * units, units), block], sems.at[block]
        )

    out_ids = lax.broadcasted_iota(jnp.int32, (BLOCK, BLOCK), 0)
    from_ids = out_ids // (2 * QUAD) * QUAD + out_ids % (2 * QUAD) // QUAD * HALF + out_ids % QUAD
    query_ids = lax.broadcasted_iota(jnp.int32, (BLOCK, BLOCK), 1)
    order_ref[...] = (from_ids == query_ids).astype(jnp.bfloat16)

    def finish(slot):
        order = order_ref[...]
        for h in range(heads):
            placed = lax.dot_general(
                order,
                acc_ref[:, h * BLOCK : (h + 1) * BLOCK],
                (((1,), (1,)), ((), ())),
                preferred_element_type=jnp.float32,
            )
            result_ref[slot, h * quads : (h + 1) * quads] = placed.reshape(
                quads, 2 * QUAD, HEAD_WIDTH
            ).astype(jnp.bfloat16)

    sizes = [min(n, before + 1) for n in range(STEP, blocks + STEP, STEP)]

    def first_of(block, size):
        return pl.multiple_of((before + block + 1 - size) * BLOCK, BLOCK)

    def score(block, length, size):
        row = pl.multiple_of(block * BLOCK, BLOCK)
        q = jnp.concatenate(
            [
                q_ref[pl.ds(row, BLOCK), pl.ds(first_lane + h * HEAD_WIDTH, HEAD_WIDTH)]
                for h in range(heads)
            ],
            axis=0,
        )
        keys = key_ref[pl.ds(first_of(block, size), size * BLOCK), :]
        s = lax.dot_general(keys, q, (((1,), (1,)), ((), ())), preferred_element_type=jnp.float32)
        pieces = [s[n * BLOCK : (n + 1) * BLOCK] for n in range(size)]
        for n in range(min(STEP, size) - 1):
            pieces[n] = jnp.where(size - n <= length, pieces[n], MASKED)
        key_ids = lax.broadcasted_iota(jnp.int32, (BLOCK, rows), 0)
        query_ids = lax.broadcasted_iota(jnp.int32, (BLOCK, rows), 1) % BLOCK
        pieces[-1] = jnp.where(key_ids <= query_ids, pieces[-1], MASKED)
        slot = block % 2
        for n in range(size):
            score_ref[slot, n * BLOCK : (n + 1) * BLOCK] = pieces[n]
        top_ref[slot] = functools.reduce(jnp.maximum, [fold(piece, jnp.max) for piece in pieces])

    def weigh(block, size):
        slot = block % 2
        shift = jnp.max(top_ref[slot], axis=0, keepdims=True) * EXP2_SCALE
        pieces = [
            jnp.exp2(score_ref[slot, n * BLOCK : (n + 1) * BLOCK] * EXP2_SCALE - shift)
            for n in range(size)
        ]
        total = functools.reduce(jnp.add, [fold(piece, jnp.sum) for piece in pieces])
        total = jnp.sum(total, axis=0, keepdims=True)
        weights = jnp.concatenate([piece.astype(jnp.bfloat16) for piece in pieces], axis=0)
        at = before + block + 1 - size
        vals = jnp.concatenate([turned_ref[at + n] for n in range(size)], axis=1)
        out = jnp.dot(vals, weights, preferred_element_type=jnp.float32)
        acc_ref[...] = (out * (1.0 / total)).astype(jnp.bfloat16)

    def fits(length, size):
        return (length > size - STEP) & (length <= size)

    for size in sizes:

        @pl.when(fits(lengths[0], size))
        def _():
            score(0, lengths[0], size)

    load.wait()

    def step(block, carry):
        length = lengths[block]
        earlier = lengths[block - 1]
        for size in sizes:
            for earlier_size in sizes:

                @pl.when(fits(length, size) & fits(earlier, earlier_size))
                def _():
                    finish(block - 1)
                    weigh(block - 1, earlier_size)
                    score(block, length, size)

        @pl.when(block > 1)
        def _():
            store_of(block - 2).start()

        return carry

    lax.fori_loop(1, blocks, step, 0)
    finish(blocks - 1)
    store_of(blocks - 2).start()
    for size in sizes:

        @pl.when(fits(lengths[blocks - 1], size))
        def _():
            weigh(blocks - 1, size)

    finish(blocks)
    store_of(blocks - 1).start()
    for block in range(blocks):
        store_of(block).wait()


def attend(lengths, q, first_lane, heads, keys, turned, earlier=None):
    blocks = q.shape[0] // BLOCK
    units = HALF // QUAD * heads
    rows = heads * BLOCK
    vmem = pl.BlockSpec(memory_space=pltpu.VMEM)
    hbm = pl.BlockSpec(memory_space=pl.ANY)
    tile = (2 * QUAD, HEAD_WIDTH)
    chained = earlier is not None
    return pl.pallas_call(
        functools.partial(attend_kernel, first_lane=first_lane, part=int(chained)),
        out_shape=jax.ShapeDtypeStruct((2 * units, blocks) + tile, jnp.bfloat16),
        in_specs=[pl.BlockSpec(memory_space=pltpu.SMEM), vmem, vmem, hbm] + [hbm] * chained,
        out_specs=hbm,
        scratch_shapes=[
            pltpu.VMEM(turned.shape, turned.dtype),
            pltpu.VMEM((BLOCK, BLOCK), jnp.bfloat16),
            pltpu.VMEM((2, blocks * BLOCK, rows), jnp.float32),
            pltpu.VMEM((2, 8, rows), jnp.float32),
            pltpu.VMEM((HEAD_WIDTH, rows), jnp.bfloat16),
            pltpu.VMEM((blocks + 1, units) + tile, jnp.bfloat16),
            pltpu.SemaphoreType.DMA(()),
            pltpu.SemaphoreType.DMA((blocks,)),
        ],
        input_output_aliases={4: 0} if chained else {},
        compiler_params=pltpu.CompilerParams(vmem_limit_bytes=20 << 20),
        name="attend_second" if chained else "attend_first",
    )(lengths, q, keys, turned, *([earlier] if chained else []))


def route_kernel(index, x_ref, y_ref):
    def step(n, carry):
        for u in range(16):
            y_ref[n * 16 + u] = x_ref[index[n * 16 + u]]
        return carry

    lax.fori_loop(0, y_ref.shape[0] // 16, step, 0)


def route(index, x):
    vmem = pl.BlockSpec(memory_space=pltpu.VMEM)
    return pl.pallas_call(
        route_kernel,
        out_shape=jax.ShapeDtypeStruct(x.shape, x.dtype),
        in_specs=[pl.BlockSpec(memory_space=pltpu.SMEM), vmem],
        out_specs=vmem,
        compiler_params=pltpu.CompilerParams(vmem_limit_bytes=8 << 20),
        name="route",
    )(index, x)


def settle_kernel(x_ref, y_ref):
    heads, quads, groups, parts = x_ref.shape[:4]

    def step(n, carry):
        half = n % 2
        pair = n // 2
        for p in range(parts):
            for g in range(groups):
                for h in range(heads):
                    y_ref[p * (quads // 2) + pair, g * heads + h, half] = x_ref[h, n, g, p]
        return carry

    lax.fori_loop(0, quads, step, 0)


def settle(x):
    heads, quads, groups, parts = x.shape[:4]
    vmem = pl.BlockSpec(memory_space=pltpu.VMEM)
    return pl.pallas_call(
        settle_kernel,
        out_shape=jax.ShapeDtypeStruct(
            (parts * quads // 2, groups * heads, 2) + x.shape[4:], x.dtype
        ),
        in_specs=[vmem],
        out_specs=vmem,
        compiler_params=pltpu.CompilerParams(vmem_limit_bytes=8 << 20),
        name="settle",
    )(x)


def on_device(queries, keys, values, doc_start, doc_blocks, doc_rank, doc_slot):
    ctx_count = lax.axis_size("ctx")
    head_count = lax.axis_size("head")
    rank_index = lax.axis_index("ctx")
    tokens = queries.shape[0]
    rows_per_rank = tokens * head_count
    blocks = rows_per_rank // BLOCK
    key_width = keys.shape[1] // head_count
    query_width = queries.shape[1] // head_count
    heads = query_width // HEAD_WIDTH


    def gather_heads(x):
        x = lax.all_to_all(x, "head", split_axis=0, concat_axis=0, tiled=True)
        return x.reshape(rows_per_rank, x.shape[2])

    half_width = query_width // 2
    firsts = gather_heads(
        pack(
            (keys, values, queries),
            ((0, key_width), (0, key_width), (0, half_width)),
            head_count,
        )
    )
    halo = lax.ppermute(
        firsts[BLOCK:, : 2 * key_width],
        "ctx",
        [(i, (i + 1) % ctx_count) for i in range(ctx_count)],
    )
    q_second = gather_heads(pack((queries,), ((half_width, half_width),), head_count))
    keys, turned = prepare(firsts, halo)

    own_blocks = rank_index * blocks + jnp.arange(blocks, dtype=jnp.int32)
    holds = (doc_start[None, :] <= own_blocks[:, None]) & (
        own_blocks[:, None] < (doc_start + doc_blocks)[None, :]
    )
    lengths = own_blocks + 1 - jnp.sum(jnp.where(holds, doc_start[None, :], 0), axis=1)

    new_blocks = jnp.arange(ctx_count * blocks, dtype=jnp.int32)
    first_new = doc_rank * blocks + doc_slot
    lands = (first_new[None, :] <= new_blocks[:, None]) & (
        new_blocks[:, None] < (first_new + doc_blocks)[None, :]
    )
    sources = new_blocks + jnp.sum(
        jnp.where(lands, (doc_start - first_new)[None, :], 0), axis=1
    )

    done = attend(lengths, firsts, 2 * key_width, heads // 2, keys, turned)
    dealt = attend(lengths, q_second, 0, heads // 2, keys, turned, done)
    dealt = lax.all_to_all(dealt, "ctx", split_axis=0, concat_axis=0, tiled=True)
    dealt = dealt.reshape(ctx_count * blocks, 2 * QUAD, HEAD_WIDTH)
    moved = route(sources, dealt)
    parts = tokens // HALF
    moved = moved.reshape(ctx_count * head_count, parts, QUAD, HEAD_WIDTH)
    placed = lax.all_to_all(moved, ("ctx", "head"), split_axis=0, concat_axis=0, tiled=True)
    placed = placed.reshape(heads, HALF // QUAD, head_count, parts, QUAD, HEAD_WIDTH)
    settled = settle(placed)
    settled = settled.reshape(settled.shape[:2] + (2 * QUAD, HEAD_WIDTH))
    return settled.transpose(0, 2, 1, 3).reshape(tokens, queries.shape[1])


def solution(mesh):
    return jax.shard_map(
        on_device,
        mesh=mesh,
        in_specs=(
            P(("ctx", "head"), None),
            P(("ctx", "head"), None),
            P(("ctx", "head"), None),
            P(),
            P(),
            P(),
            P(),
        ),
        out_specs=P(("ctx", "head"), None),
        check_vma=False,
    )
```

```python
import functools
import math

import jax
import jax.numpy as jnp
from jax import lax
from jax.experimental import pallas as pl
from jax.experimental.pallas import tpu as pltpu
from jax.sharding import PartitionSpec as P

HEAD_WIDTH = 128
BLOCK = 128
HALF = 64
QUAD = 4
STEP = 4
LEAD_HEADS = 1
MASKED = -1e30
EXP2_SCALE = math.log2(math.e) / math.sqrt(HEAD_WIDTH)


def pack_kernel(*refs, pieces):
    out_hbm, packed_ref, in_sems, out_sems = refs[-4:]
    groups = out_hbm.shape[0]
    loads = []
    stores = []
    for g in range(groups):
        at = 0
        for n, (start, width) in enumerate(pieces):
            source = refs[n]
            first = g * (source.shape[1] // groups) + start
            loads.append(
                pltpu.make_async_copy(
                    source.at[:, pl.ds(first, width)],
                    packed_ref.at[g, :, pl.ds(at, width)],
                    in_sems.at[g, n],
                )
            )
            at += width
        stores.append(pltpu.make_async_copy(packed_ref.at[g], out_hbm.at[g], out_sems.at[g]))
    for load in loads:
        load.start()
    for g in range(groups):
        for load in loads[g * len(pieces) : (g + 1) * len(pieces)]:
            load.wait()
        stores[g].start()
    for store in stores:
        store.wait()


def pack(arrays, pieces, groups):
    tokens = arrays[0].shape[0]
    shape = (groups, tokens, sum(width for _, width in pieces))
    return pl.pallas_call(
        functools.partial(pack_kernel, pieces=pieces),
        out_shape=jax.ShapeDtypeStruct(shape, arrays[0].dtype),
        in_specs=[pl.BlockSpec(memory_space=pl.ANY)] * len(arrays),
        out_specs=pl.BlockSpec(memory_space=pl.ANY),
        scratch_shapes=[
            pltpu.VMEM(shape, arrays[0].dtype),
            pltpu.SemaphoreType.DMA((groups, len(arrays))),
            pltpu.SemaphoreType.DMA((groups,)),
        ],
        name="pack",
    )(*arrays)


def prepare_kernel(kv_ref, halo_hbm, key_ref, turned_ref, halo_ref, sem):
    before = halo_ref.shape[0]
    load = pltpu.make_async_copy(halo_hbm, halo_ref, sem)
    load.start()

    def place(source_ref, at):
        key_ref[pl.ds(at, source_ref.shape[0]), :] = source_ref[:, :HEAD_WIDTH]

        def turn(n, carry):
            first = pl.multiple_of(n * BLOCK, BLOCK)
            part = source_ref[pl.ds(first, BLOCK), HEAD_WIDTH : 2 * HEAD_WIDTH].astype(jnp.float32)
            turned_ref[at // BLOCK + n] = part.T.astype(jnp.bfloat16)
            return carry

        lax.fori_loop(0, source_ref.shape[0] // BLOCK, turn, 0)

    place(kv_ref, before)
    load.wait()
    place(halo_ref, 0)


def prepare(kv, halo):
    window = kv.shape[0] + halo.shape[0]
    vmem = pl.BlockSpec(memory_space=pltpu.VMEM)
    return pl.pallas_call(
        prepare_kernel,
        out_shape=(
            jax.ShapeDtypeStruct((window, HEAD_WIDTH), kv.dtype),
            jax.ShapeDtypeStruct((window // BLOCK, HEAD_WIDTH, BLOCK), kv.dtype),
        ),
        in_specs=[vmem, pl.BlockSpec(memory_space=pl.ANY)],
        out_specs=(vmem, vmem),
        scratch_shapes=[pltpu.VMEM(halo.shape, halo.dtype), pltpu.SemaphoreType.DMA(())],
        compiler_params=pltpu.CompilerParams(vmem_limit_bytes=8 << 20),
        name="prepare",
    )(kv, halo)


def attend_kernel(lengths, q_ref, key_ref, turned_hbm, *refs, first_lane, first_head):
    out_hbm, turned_ref, order_ref, score_ref, top_ref, acc_ref, result_ref, load_sem, sems = refs[-9:]
    load = pltpu.make_async_copy(turned_hbm, turned_ref, load_sem)
    load.start()
    units = result_ref.shape[1]
    quads = HALF // QUAD
    heads = units // quads
    rows = heads * BLOCK
    blocks = q_ref.shape[0] // BLOCK
    before = key_ref.shape[0] // BLOCK - blocks

    def fold(x, op):
        return op(x.reshape(BLOCK // 8, 8, rows), axis=0)

    def store_of(block):
        return pltpu.make_async_copy(
            result_ref.at[block + 1],
            out_hbm.at[pl.ds(first_head * quads, units), block],
            sems.at[block],
        )

    out_ids = lax.broadcasted_iota(jnp.int32, (BLOCK, BLOCK), 0)
    from_ids = out_ids // (2 * QUAD) * QUAD + out_ids % (2 * QUAD) // QUAD * HALF + out_ids % QUAD
    query_ids = lax.broadcasted_iota(jnp.int32, (BLOCK, BLOCK), 1)
    order_ref[...] = (from_ids == query_ids).astype(jnp.bfloat16)

    def finish(slot):
        order = order_ref[...]
        for h in range(heads):
            placed = lax.dot_general(
                order,
                acc_ref[:, h * BLOCK : (h + 1) * BLOCK],
                (((1,), (1,)), ((), ())),
                preferred_element_type=jnp.float32,
            )
            result_ref[slot, h * quads : (h + 1) * quads] = placed.reshape(
                quads, 2 * QUAD, HEAD_WIDTH
            ).astype(jnp.bfloat16)

    sizes = [min(n, before + 1) for n in range(STEP, blocks + STEP, STEP)]

    def first_of(block, size):
        return pl.multiple_of((before + block + 1 - size) * BLOCK, BLOCK)

    def score(block, length, size):
        row = pl.multiple_of(block * BLOCK, BLOCK)
        q = jnp.concatenate(
            [
                q_ref[pl.ds(row, BLOCK), pl.ds(first_lane + h * HEAD_WIDTH, HEAD_WIDTH)]
                for h in range(heads)
            ],
            axis=0,
        )
        keys = key_ref[pl.ds(first_of(block, size), size * BLOCK), :]
        s = lax.dot_general(keys, q, (((1,), (1,)), ((), ())), preferred_element_type=jnp.float32)
        pieces = [s[n * BLOCK : (n + 1) * BLOCK] for n in range(size)]
        for n in range(min(STEP, size) - 1):
            pieces[n] = jnp.where(size - n <= length, pieces[n], MASKED)
        key_ids = lax.broadcasted_iota(jnp.int32, (BLOCK, rows), 0)
        query_ids = lax.broadcasted_iota(jnp.int32, (BLOCK, rows), 1) % BLOCK
        pieces[-1] = jnp.where(key_ids <= query_ids, pieces[-1], MASKED)
        slot = block % 2
        for n in range(size):
            score_ref[slot, n * BLOCK : (n + 1) * BLOCK] = pieces[n]
        top_ref[slot] = functools.reduce(jnp.maximum, [fold(piece, jnp.max) for piece in pieces])

    def weigh(block, size):
        slot = block % 2
        shift = jnp.max(top_ref[slot], axis=0, keepdims=True) * EXP2_SCALE
        pieces = [
            jnp.exp2(score_ref[slot, n * BLOCK : (n + 1) * BLOCK] * EXP2_SCALE - shift)
            for n in range(size)
        ]
        total = functools.reduce(jnp.add, [fold(piece, jnp.sum) for piece in pieces])
        total = jnp.sum(total, axis=0, keepdims=True)
        weights = jnp.concatenate([piece.astype(jnp.bfloat16) for piece in pieces], axis=0)
        at = before + block + 1 - size
        vals = jnp.concatenate([turned_ref[at + n] for n in range(size)], axis=1)
        out = jnp.dot(vals, weights, preferred_element_type=jnp.float32)
        acc_ref[...] = (out * (1.0 / total)).astype(jnp.bfloat16)

    def fits(length, size):
        return (length > size - STEP) & (length <= size)

    for size in sizes:

        @pl.when(fits(lengths[0], size))
        def _():
            score(0, lengths[0], size)

    load.wait()

    def step(block, carry):
        length = lengths[block]
        earlier = lengths[block - 1]
        for size in sizes:
            for earlier_size in sizes:

                @pl.when(fits(length, size) & fits(earlier, earlier_size))
                def _():
                    finish(block - 1)
                    weigh(block - 1, earlier_size)
                    score(block, length, size)

        @pl.when(block > 1)
        def _():
            store_of(block - 2).start()

        return carry

    lax.fori_loop(1, blocks, step, 0)
    finish(blocks - 1)
    store_of(blocks - 2).start()
    for size in sizes:

        @pl.when(fits(lengths[blocks - 1], size))
        def _():
            weigh(blocks - 1, size)

    finish(blocks)
    store_of(blocks - 1).start()
    for block in range(blocks):
        store_of(block).wait()


def attend(lengths, q, first_lane, first_head, heads, all_heads, keys, turned, earlier=None):
    blocks = q.shape[0] // BLOCK
    units = HALF // QUAD * heads
    rows = heads * BLOCK
    vmem = pl.BlockSpec(memory_space=pltpu.VMEM)
    hbm = pl.BlockSpec(memory_space=pl.ANY)
    tile = (2 * QUAD, HEAD_WIDTH)
    chained = earlier is not None
    return pl.pallas_call(
        functools.partial(attend_kernel, first_lane=first_lane, first_head=first_head),
        out_shape=jax.ShapeDtypeStruct((HALF // QUAD * all_heads, blocks) + tile, jnp.bfloat16),
        in_specs=[pl.BlockSpec(memory_space=pltpu.SMEM), vmem, vmem, hbm] + [hbm] * chained,
        out_specs=hbm,
        scratch_shapes=[
            pltpu.VMEM(turned.shape, turned.dtype),
            pltpu.VMEM((BLOCK, BLOCK), jnp.bfloat16),
            pltpu.VMEM((2, blocks * BLOCK, rows), jnp.float32),
            pltpu.VMEM((2, 8, rows), jnp.float32),
            pltpu.VMEM((HEAD_WIDTH, rows), jnp.bfloat16),
            pltpu.VMEM((blocks + 1, units) + tile, jnp.bfloat16),
            pltpu.SemaphoreType.DMA(()),
            pltpu.SemaphoreType.DMA((blocks,)),
        ],
        input_output_aliases={4: 0} if chained else {},
        compiler_params=pltpu.CompilerParams(vmem_limit_bytes=20 << 20),
        name="attend_second" if chained else "attend_first",
    )(lengths, q, keys, turned, *([earlier] if chained else []))


def route_kernel(index, x_ref, y_ref):
    def step(n, carry):
        for u in range(16):
            y_ref[n * 16 + u] = x_ref[index[n * 16 + u]]
        return carry

    lax.fori_loop(0, y_ref.shape[0] // 16, step, 0)


def route(index, x):
    vmem = pl.BlockSpec(memory_space=pltpu.VMEM)
    return pl.pallas_call(
        route_kernel,
        out_shape=jax.ShapeDtypeStruct(x.shape, x.dtype),
        in_specs=[pl.BlockSpec(memory_space=pltpu.SMEM), vmem],
        out_specs=vmem,
        compiler_params=pltpu.CompilerParams(vmem_limit_bytes=8 << 20),
        name="route",
    )(index, x)


def settle_kernel(x_ref, y_ref):
    heads, quads, groups, parts = x_ref.shape[:4]

    def step(n, carry):
        half = n % 2
        pair = n // 2
        for p in range(parts):
            for g in range(groups):
                for h in range(heads):
                    y_ref[p * (quads // 2) + pair, g * heads + h, half] = x_ref[h, n, g, p]
        return carry

    lax.fori_loop(0, quads, step, 0)


def settle(x):
    heads, quads, groups, parts = x.shape[:4]
    vmem = pl.BlockSpec(memory_space=pltpu.VMEM)
    return pl.pallas_call(
        settle_kernel,
        out_shape=jax.ShapeDtypeStruct(
            (parts * quads // 2, groups * heads, 2) + x.shape[4:], x.dtype
        ),
        in_specs=[vmem],
        out_specs=vmem,
        compiler_params=pltpu.CompilerParams(vmem_limit_bytes=8 << 20),
        name="settle",
    )(x)


def on_device(queries, keys, values, doc_start, doc_blocks, doc_rank, doc_slot):
    ctx_count = lax.axis_size("ctx")
    head_count = lax.axis_size("head")
    rank_index = lax.axis_index("ctx")
    tokens = queries.shape[0]
    rows_per_rank = tokens * head_count
    blocks = rows_per_rank // BLOCK
    key_width = keys.shape[1] // head_count
    query_width = queries.shape[1] // head_count
    heads = query_width // HEAD_WIDTH


    def gather_heads(x):
        x = lax.all_to_all(x, "head", split_axis=0, concat_axis=0, tiled=True)
        return x.reshape(rows_per_rank, x.shape[2])

    lead = LEAD_HEADS * HEAD_WIDTH
    rest = query_width - lead
    firsts = gather_heads(
        pack(
            (keys, values, queries),
            ((0, key_width), (0, key_width), (0, lead)),
            head_count,
        )
    )
    halo = lax.ppermute(
        firsts[BLOCK:, : 2 * key_width],
        "ctx",
        [(i, (i + 1) % ctx_count) for i in range(ctx_count)],
    )
    q_second = gather_heads(pack((queries,), ((lead, rest),), head_count))
    keys, turned = prepare(firsts, halo)

    own_blocks = rank_index * blocks + jnp.arange(blocks, dtype=jnp.int32)
    holds = (doc_start[None, :] <= own_blocks[:, None]) & (
        own_blocks[:, None] < (doc_start + doc_blocks)[None, :]
    )
    lengths = own_blocks + 1 - jnp.sum(jnp.where(holds, doc_start[None, :], 0), axis=1)

    new_blocks = jnp.arange(ctx_count * blocks, dtype=jnp.int32)
    first_new = doc_rank * blocks + doc_slot
    lands = (first_new[None, :] <= new_blocks[:, None]) & (
        new_blocks[:, None] < (first_new + doc_blocks)[None, :]
    )
    sources = new_blocks + jnp.sum(
        jnp.where(lands, (doc_start - first_new)[None, :], 0), axis=1
    )

    done = attend(lengths, firsts, 2 * key_width, 0, LEAD_HEADS, heads, keys, turned)
    dealt = attend(
        lengths, q_second, 0, LEAD_HEADS, heads - LEAD_HEADS, heads, keys, turned, done
    )
    dealt = lax.all_to_all(dealt, "ctx", split_axis=0, concat_axis=0, tiled=True)
    dealt = dealt.reshape(ctx_count * blocks, 2 * QUAD, HEAD_WIDTH)
    moved = route(sources, dealt)
    parts = tokens // HALF
    moved = moved.reshape(ctx_count * head_count, parts, QUAD, HEAD_WIDTH)
    placed = lax.all_to_all(moved, ("ctx", "head"), split_axis=0, concat_axis=0, tiled=True)
    placed = placed.reshape(heads, HALF // QUAD, head_count, parts, QUAD, HEAD_WIDTH)
    settled = settle(placed)
    settled = settled.reshape(settled.shape[:2] + (2 * QUAD, HEAD_WIDTH))
    return settled.transpose(0, 2, 1, 3).reshape(tokens, queries.shape[1])


def solution(mesh):
    return jax.shard_map(
        on_device,
        mesh=mesh,
        in_specs=(
            P(("ctx", "head"), None),
            P(("ctx", "head"), None),
            P(("ctx", "head"), None),
            P(),
            P(),
            P(),
            P(),
        ),
        out_specs=P(("ctx", "head"), None),
        check_vma=False,
    )
```

```python
import functools
import math

import jax
import jax.numpy as jnp
from jax import lax
from jax.experimental import pallas as pl
from jax.experimental.pallas import tpu as pltpu
from jax.sharding import PartitionSpec as P

HEAD_WIDTH = 128
BLOCK = 128
HALF = 64
QUAD = 4
STEP = 3
LEAD_HEADS = 1
MASKED = -1e30
EXP2_SCALE = math.log2(math.e) / math.sqrt(HEAD_WIDTH)


def pack_kernel(*refs, pieces):
    out_hbm, packed_ref, in_sems, out_sems = refs[-4:]
    groups = out_hbm.shape[0]
    loads = []
    stores = []
    for g in range(groups):
        at = 0
        for n, (start, width) in enumerate(pieces):
            source = refs[n]
            first = g * (source.shape[1] // groups) + start
            loads.append(
                pltpu.make_async_copy(
                    source.at[:, pl.ds(first, width)],
                    packed_ref.at[g, :, pl.ds(at, width)],
                    in_sems.at[g, n],
                )
            )
            at += width
        stores.append(pltpu.make_async_copy(packed_ref.at[g], out_hbm.at[g], out_sems.at[g]))
    for load in loads:
        load.start()
    for g in range(groups):
        for load in loads[g * len(pieces) : (g + 1) * len(pieces)]:
            load.wait()
        stores[g].start()
    for store in stores:
        store.wait()


def pack(arrays, pieces, groups):
    tokens = arrays[0].shape[0]
    shape = (groups, tokens, sum(width for _, width in pieces))
    return pl.pallas_call(
        functools.partial(pack_kernel, pieces=pieces),
        out_shape=jax.ShapeDtypeStruct(shape, arrays[0].dtype),
        in_specs=[pl.BlockSpec(memory_space=pl.ANY)] * len(arrays),
        out_specs=pl.BlockSpec(memory_space=pl.ANY),
        scratch_shapes=[
            pltpu.VMEM(shape, arrays[0].dtype),
            pltpu.SemaphoreType.DMA((groups, len(arrays))),
            pltpu.SemaphoreType.DMA((groups,)),
        ],
        name="pack",
    )(*arrays)


def prepare_kernel(kv_ref, halo_hbm, key_ref, turned_ref, halo_ref, sem):
    before = halo_ref.shape[0]
    load = pltpu.make_async_copy(halo_hbm, halo_ref, sem)
    load.start()

    def place(source_ref, at):
        key_ref[pl.ds(at, source_ref.shape[0]), :] = source_ref[:, :HEAD_WIDTH]

        def turn(n, carry):
            first = pl.multiple_of(n * BLOCK, BLOCK)
            part = source_ref[pl.ds(first, BLOCK), HEAD_WIDTH : 2 * HEAD_WIDTH].astype(jnp.float32)
            turned_ref[at // BLOCK + n] = part.T.astype(jnp.bfloat16)
            return carry

        lax.fori_loop(0, source_ref.shape[0] // BLOCK, turn, 0)

    place(kv_ref, before)
    load.wait()
    place(halo_ref, 0)


def prepare(kv, halo):
    window = kv.shape[0] + halo.shape[0]
    vmem = pl.BlockSpec(memory_space=pltpu.VMEM)
    return pl.pallas_call(
        prepare_kernel,
        out_shape=(
            jax.ShapeDtypeStruct((window, HEAD_WIDTH), kv.dtype),
            jax.ShapeDtypeStruct((window // BLOCK, HEAD_WIDTH, BLOCK), kv.dtype),
        ),
        in_specs=[vmem, pl.BlockSpec(memory_space=pl.ANY)],
        out_specs=(vmem, vmem),
        scratch_shapes=[pltpu.VMEM(halo.shape, halo.dtype), pltpu.SemaphoreType.DMA(())],
        compiler_params=pltpu.CompilerParams(vmem_limit_bytes=8 << 20),
        name="prepare",
    )(kv, halo)


def attend_kernel(lengths, q_ref, key_ref, turned_hbm, *refs, first_lane, first_head):
    out_hbm, turned_ref, order_ref, score_ref, top_ref, acc_ref, result_ref, load_sem, sems = refs[-9:]
    load = pltpu.make_async_copy(turned_hbm, turned_ref, load_sem)
    load.start()
    units = result_ref.shape[1]
    quads = HALF // QUAD
    heads = units // quads
    rows = heads * BLOCK
    blocks = q_ref.shape[0] // BLOCK
    before = key_ref.shape[0] // BLOCK - blocks

    def fold(x, op):
        return op(x.reshape(BLOCK // 8, 8, rows), axis=0)

    def store_of(block):
        return pltpu.make_async_copy(
            result_ref.at[block + 1],
            out_hbm.at[pl.ds(first_head * quads, units), block],
            sems.at[block],
        )

    out_ids = lax.broadcasted_iota(jnp.int32, (BLOCK, BLOCK), 0)
    from_ids = out_ids // (2 * QUAD) * QUAD + out_ids % (2 * QUAD) // QUAD * HALF + out_ids % QUAD
    query_ids = lax.broadcasted_iota(jnp.int32, (BLOCK, BLOCK), 1)
    order_ref[...] = (from_ids == query_ids).astype(jnp.bfloat16)

    def finish(slot):
        order = order_ref[...]
        for h in range(heads):
            placed = lax.dot_general(
                order,
                acc_ref[:, h * BLOCK : (h + 1) * BLOCK],
                (((1,), (1,)), ((), ())),
                preferred_element_type=jnp.float32,
            )
            result_ref[slot, h * quads : (h + 1) * quads] = placed.reshape(
                quads, 2 * QUAD, HEAD_WIDTH
            ).astype(jnp.bfloat16)

    sizes = [min(n, before + 1) for n in range(STEP, blocks + STEP, STEP)]

    def first_of(block, size):
        return pl.multiple_of((before + block + 1 - size) * BLOCK, BLOCK)

    def score(block, length, size):
        row = pl.multiple_of(block * BLOCK, BLOCK)
        q = jnp.concatenate(
            [
                q_ref[pl.ds(row, BLOCK), pl.ds(first_lane + h * HEAD_WIDTH, HEAD_WIDTH)]
                for h in range(heads)
            ],
            axis=0,
        )
        keys = key_ref[pl.ds(first_of(block, size), size * BLOCK), :]
        s = lax.dot_general(keys, q, (((1,), (1,)), ((), ())), preferred_element_type=jnp.float32)
        pieces = [s[n * BLOCK : (n + 1) * BLOCK] for n in range(size)]
        for n in range(min(STEP, size) - 1):
            pieces[n] = jnp.where(size - n <= length, pieces[n], MASKED)
        key_ids = lax.broadcasted_iota(jnp.int32, (BLOCK, rows), 0)
        query_ids = lax.broadcasted_iota(jnp.int32, (BLOCK, rows), 1) % BLOCK
        pieces[-1] = jnp.where(key_ids <= query_ids, pieces[-1], MASKED)
        slot = block % 2
        for n in range(size):
            score_ref[slot, n * BLOCK : (n + 1) * BLOCK] = pieces[n]
        top_ref[slot] = functools.reduce(jnp.maximum, [fold(piece, jnp.max) for piece in pieces])

    def weigh(block, size):
        slot = block % 2
        shift = jnp.max(top_ref[slot], axis=0, keepdims=True) * EXP2_SCALE
        pieces = [
            jnp.exp2(score_ref[slot, n * BLOCK : (n + 1) * BLOCK] * EXP2_SCALE - shift)
            for n in range(size)
        ]
        total = functools.reduce(jnp.add, [fold(piece, jnp.sum) for piece in pieces])
        total = jnp.sum(total, axis=0, keepdims=True)
        weights = jnp.concatenate([piece.astype(jnp.bfloat16) for piece in pieces], axis=0)
        at = before + block + 1 - size
        vals = jnp.concatenate([turned_ref[at + n] for n in range(size)], axis=1)
        out = jnp.dot(vals, weights, preferred_element_type=jnp.float32)
        acc_ref[...] = (out * (1.0 / total)).astype(jnp.bfloat16)

    def fits(length, size):
        return (length > size - STEP) & (length <= size)

    for size in sizes:

        @pl.when(fits(lengths[0], size))
        def _():
            score(0, lengths[0], size)

    load.wait()

    def step(block, carry):
        length = lengths[block]
        earlier = lengths[block - 1]
        for size in sizes:
            for earlier_size in sizes:

                @pl.when(fits(length, size) & fits(earlier, earlier_size))
                def _():
                    finish(block - 1)
                    weigh(block - 1, earlier_size)
                    score(block, length, size)

        @pl.when(block > 1)
        def _():
            store_of(block - 2).start()

        return carry

    lax.fori_loop(1, blocks, step, 0)
    finish(blocks - 1)
    store_of(blocks - 2).start()
    for size in sizes:

        @pl.when(fits(lengths[blocks - 1], size))
        def _():
            weigh(blocks - 1, size)

    finish(blocks)
    store_of(blocks - 1).start()
    for block in range(blocks):
        store_of(block).wait()


def attend(lengths, q, first_lane, first_head, heads, all_heads, keys, turned, earlier=None):
    blocks = q.shape[0] // BLOCK
    units = HALF // QUAD * heads
    rows = heads * BLOCK
    vmem = pl.BlockSpec(memory_space=pltpu.VMEM)
    hbm = pl.BlockSpec(memory_space=pl.ANY)
    tile = (2 * QUAD, HEAD_WIDTH)
    chained = earlier is not None
    return pl.pallas_call(
        functools.partial(attend_kernel, first_lane=first_lane, first_head=first_head),
        out_shape=jax.ShapeDtypeStruct((HALF // QUAD * all_heads, blocks) + tile, jnp.bfloat16),
        in_specs=[pl.BlockSpec(memory_space=pltpu.SMEM), vmem, vmem, hbm] + [hbm] * chained,
        out_specs=hbm,
        scratch_shapes=[
            pltpu.VMEM(turned.shape, turned.dtype),
            pltpu.VMEM((BLOCK, BLOCK), jnp.bfloat16),
            pltpu.VMEM((2, blocks * BLOCK, rows), jnp.float32),
            pltpu.VMEM((2, 8, rows), jnp.float32),
            pltpu.VMEM((HEAD_WIDTH, rows), jnp.bfloat16),
            pltpu.VMEM((blocks + 1, units) + tile, jnp.bfloat16),
            pltpu.SemaphoreType.DMA(()),
            pltpu.SemaphoreType.DMA((blocks,)),
        ],
        input_output_aliases={4: 0} if chained else {},
        compiler_params=pltpu.CompilerParams(vmem_limit_bytes=20 << 20),
        name="attend_second" if chained else "attend_first",
    )(lengths, q, keys, turned, *([earlier] if chained else []))


def route_kernel(index, x_ref, y_ref):
    def step(n, carry):
        for u in range(16):
            y_ref[n * 16 + u] = x_ref[index[n * 16 + u]]
        return carry

    lax.fori_loop(0, y_ref.shape[0] // 16, step, 0)


def route(index, x):
    vmem = pl.BlockSpec(memory_space=pltpu.VMEM)
    return pl.pallas_call(
        route_kernel,
        out_shape=jax.ShapeDtypeStruct(x.shape, x.dtype),
        in_specs=[pl.BlockSpec(memory_space=pltpu.SMEM), vmem],
        out_specs=vmem,
        compiler_params=pltpu.CompilerParams(vmem_limit_bytes=8 << 20),
        name="route",
    )(index, x)


def settle_kernel(x_ref, y_ref):
    heads, quads, groups, parts = x_ref.shape[:4]

    def step(n, carry):
        half = n % 2
        pair = n // 2
        for p in range(parts):
            for g in range(groups):
                for h in range(heads):
                    y_ref[p * (quads // 2) + pair, g * heads + h, half] = x_ref[h, n, g, p]
        return carry

    lax.fori_loop(0, quads, step, 0)


def settle(x):
    heads, quads, groups, parts = x.shape[:4]
    vmem = pl.BlockSpec(memory_space=pltpu.VMEM)
    return pl.pallas_call(
        settle_kernel,
        out_shape=jax.ShapeDtypeStruct(
            (parts * quads // 2, groups * heads, 2) + x.shape[4:], x.dtype
        ),
        in_specs=[vmem],
        out_specs=vmem,
        compiler_params=pltpu.CompilerParams(vmem_limit_bytes=8 << 20),
        name="settle",
    )(x)


def on_device(queries, keys, values, doc_start, doc_blocks, doc_rank, doc_slot):
    ctx_count = lax.axis_size("ctx")
    head_count = lax.axis_size("head")
    rank_index = lax.axis_index("ctx")
    tokens = queries.shape[0]
    rows_per_rank = tokens * head_count
    blocks = rows_per_rank // BLOCK
    key_width = keys.shape[1] // head_count
    query_width = queries.shape[1] // head_count
    heads = query_width // HEAD_WIDTH


    def gather_heads(x):
        x = lax.all_to_all(x, "head", split_axis=0, concat_axis=0, tiled=True)
        return x.reshape(rows_per_rank, x.shape[2])

    lead = LEAD_HEADS * HEAD_WIDTH
    rest = query_width - lead
    firsts = gather_heads(
        pack(
            (keys, values, queries),
            ((0, key_width), (0, key_width), (0, lead)),
            head_count,
        )
    )
    halo = lax.ppermute(
        firsts[BLOCK:, : 2 * key_width],
        "ctx",
        [(i, (i + 1) % ctx_count) for i in range(ctx_count)],
    )
    q_second = gather_heads(pack((queries,), ((lead, rest),), head_count))
    keys, turned = prepare(firsts, halo)

    own_blocks = rank_index * blocks + jnp.arange(blocks, dtype=jnp.int32)
    holds = (doc_start[None, :] <= own_blocks[:, None]) & (
        own_blocks[:, None] < (doc_start + doc_blocks)[None, :]
    )
    lengths = own_blocks + 1 - jnp.sum(jnp.where(holds, doc_start[None, :], 0), axis=1)

    new_blocks = jnp.arange(ctx_count * blocks, dtype=jnp.int32)
    first_new = doc_rank * blocks + doc_slot
    lands = (first_new[None, :] <= new_blocks[:, None]) & (
        new_blocks[:, None] < (first_new + doc_blocks)[None, :]
    )
    sources = new_blocks + jnp.sum(
        jnp.where(lands, (doc_start - first_new)[None, :], 0), axis=1
    )

    done = attend(lengths, firsts, 2 * key_width, 0, LEAD_HEADS, heads, keys, turned)
    dealt = attend(
        lengths, q_second, 0, LEAD_HEADS, heads - LEAD_HEADS, heads, keys, turned, done
    )
    dealt = lax.all_to_all(dealt, "ctx", split_axis=0, concat_axis=0, tiled=True)
    dealt = dealt.reshape(ctx_count * blocks, 2 * QUAD, HEAD_WIDTH)
    moved = route(sources, dealt)
    parts = tokens // HALF
    moved = moved.reshape(ctx_count * head_count, parts, QUAD, HEAD_WIDTH)
    placed = lax.all_to_all(moved, ("ctx", "head"), split_axis=0, concat_axis=0, tiled=True)
    placed = placed.reshape(heads, HALF // QUAD, head_count, parts, QUAD, HEAD_WIDTH)
    settled = settle(placed)
    settled = settled.reshape(settled.shape[:2] + (2 * QUAD, HEAD_WIDTH))
    return settled.transpose(0, 2, 1, 3).reshape(tokens, queries.shape[1])


def solution(mesh):
    return jax.shard_map(
        on_device,
        mesh=mesh,
        in_specs=(
            P(("ctx", "head"), None),
            P(("ctx", "head"), None),
            P(("ctx", "head"), None),
            P(),
            P(),
            P(),
            P(),
        ),
        out_specs=P(("ctx", "head"), None),
        check_vma=False,
    )
```
